512 devices in a mesh: lon: 16 (over z), lat: 8 (over x_lo, y), ch: 4 (over x_hi, core).
Axes of the slice: x: 4 (x_hi: 2, x_lo: 2; x = x_hi * 2 + x_lo), y: 4, z: 16, core: 2. Of those that a mesh axis runs over, the one named last changes fastest.
Arguments:
- ocean_state: bfloat16 [300, 256, 2048], P('ch', 'lat', 'lon'), may hold values from -6 to 6
- land_mask: int32 [256, 2048], P('lat', 'lon'), may hold values 0 or 1
- out_grad: bfloat16 [300, 256, 2048], P('ch', 'lat', 'lon'), may hold values from -6 to 6
- swath_offset: int32 [8, 16, 512], P('lat', 'lon'), may hold values from 0 to 4095
- swath_value: float32 [8, 16, 512], P('lat', 'lon'), may hold values from -8 to 8
- depth_kernel: float32 [3, 3, 300], P(None, None, 'ch'), may hold values from -2.5 to 2.5
- expand_weight: bfloat16 [300, 600], P(None, 'ch'), may hold values from -0.375 to 0.375
- expand_bias: float32 [600], P('ch'), may hold values from -3 to 3
- project_weight: bfloat16 [600, 300], P('ch'), may hold values from -0.25 to 0.25
Outputs:
- state_grad: bfloat16 [300, 256, 2048], P('ch', 'lat', 'lon')
- expand_grad: float32 [300, 600], P(None, 'ch')
- project_grad: float32 [600, 300], P('ch')
- bias_grad: float32 [600], P('ch')
- kernel_grad: float32 [3, 3, 300], P(None, None, 'ch')
The draws below stay inside these ranges and needn't reach their ends.
Inputs may be any that keep to these rules, and one draw needn't show every extreme that they name: `swath_offset`: position of a swath point in row-major order over the 32 x 128 cells of its device's block.
All inputs are finite; a program needn't handle non-finite values. No bound on the sum of `land_mask` on one device may be relied on, other than what follows from the above.
Results may differ from the reference program's by a relative error of at most 0.014.
Values may be sent and summed in bfloat16 or wider, within the bound.
A program may use at most 64 MiB of HBM per device.

```python
import jax
import jax.numpy as jnp
from jax import lax

C = 300
HID = 600
DILATION_STEP = 2
ROWS = 32
COLS = 128
SWATH = 512
GRID_ROWS = 256
GRID_COLUMNS = 2048
N_LON = 16
N_LAT = 8
N_CH = 4


def plant(drawn, key, smallest, high):
    longest = drawn.shape.index(max(drawn.shape))
    spots = []
    for shift in (0, 1):
        where = [jax.random.randint(jax.random.fold_in(key, axis), (), 0, length) for axis, length in enumerate(drawn.shape)]
        where[longest] = (where[longest] + shift) % drawn.shape[longest]
        spots.append(tuple(where))
    return drawn.at[spots[0]].set(smallest).at[spots[1]].set(high)


def block_levels(rng, extent, split, least, top_value):
    def one(dim, shards_of):
        draws = jax.random.uniform(jax.random.fold_in(jax.random.fold_in(rng, 6), dim), (shards_of,), jnp.float32, least / len(split), top_value / len(split))
        return jnp.repeat(jnp.exp(draws), extent[dim] // shards_of).reshape((-1,) + (1,) * (len(extent) - dim - 1))

    factor_of = one(*split[0])
    for cut in split[1:]:
        factor_of = factor_of * one(*cut)
    return factor_of


def normal_values(own_key, dims, width, most, shards=(), kind=jnp.bfloat16):
    array = jax.random.normal(own_key, dims, jnp.float32) * width
    if len(shards) > 0:
        array = block_levels(own_key, dims, shards, -0.22, 0.18) * array
    return jnp.clip(array, min=-most, max=most).astype(kind)


def setup_inputs(seed: int = 0) -> dict:
    key_list = jax.random.split(jax.random.key(seed), 10)
    return {
        "ocean_state": normal_values(key_list[0], (C, GRID_ROWS, GRID_COLUMNS), 1.0, 6.0, ((0, 4), (1, 8), (2, 16))),
        "land_mask": plant((jax.random.randint(key_list[1], (GRID_ROWS, GRID_COLUMNS), 0, 4) < 3).astype(jnp.int32), jax.random.fold_in(key_list[1], 1), 0, 1),
        "out_grad": normal_values(key_list[2], (C, GRID_ROWS, GRID_COLUMNS), 1.0, 6.0, ((0, 4), (1, 8), (2, 16))),
        "swath_offset": plant(jax.random.randint(key_list[3], (N_LAT, N_LON, SWATH), 0, ROWS * COLS), jax.random.fold_in(key_list[3], 1), 0, (ROWS * COLS) - 1).astype(jnp.int32),
        "swath_value": normal_values(key_list[4], (N_LAT, N_LON, SWATH), 2.0, 8.0, ((0, 8), (1, 16)), jnp.float32),
        "depth_kernel": normal_values(key_list[5], (3, 3, C), 0.4, 2.5, ((2, 4),), jnp.float32),
        "expand_weight": normal_values(key_list[6], (C, HID), C ** -0.5, 0.375, ((1, 4),)),
        "expand_bias": normal_values(key_list[7], (HID,), 0.5, 3.0, ((0, 4),), jnp.float32),
        "project_weight": normal_values(key_list[8], (HID, C), HID ** -0.5, 0.25, ((0, 4),)),
    }


def pad_grid(ocean_field):
    longitude_wrapped = jnp.concatenate([ocean_field[:, -DILATION_STEP:], ocean_field, ocean_field[:, :DILATION_STEP]], axis=1)
    seam_folded = ocean_field[GRID_ROWS - DILATION_STEP:, :][::-1, ::-1]
    seam_folded = jnp.concatenate([seam_folded[:, -DILATION_STEP:], seam_folded, seam_folded[:, :DILATION_STEP]], axis=1)
    southern_rows = jnp.zeros((DILATION_STEP, GRID_COLUMNS + 2 * DILATION_STEP), ocean_field.dtype)
    return jnp.concatenate([southern_rows, longitude_wrapped, seam_folded], axis=0)

def conv_plane(ocean_field, taps):
    halo_padded = pad_grid(ocean_field)
    total = jnp.zeros((GRID_ROWS, GRID_COLUMNS), ocean_field.dtype)
    for row_offset in range(3):
        for column_offset in range(3):
            kernel_window = halo_padded[DILATION_STEP * row_offset:DILATION_STEP * row_offset + GRID_ROWS, DILATION_STEP * column_offset:DILATION_STEP * column_offset + GRID_COLUMNS]
            total = total + taps[row_offset, column_offset] * kernel_window
    return total

def reference(ocean_state, land_mask, out_grad, swath_offset, swath_value, depth_kernel, expand_weight, expand_bias, project_weight):
    mask_float = land_mask.astype(jnp.float32)
    masked = ocean_state * land_mask.astype(jnp.bfloat16)[None]
    kernels = jnp.moveaxis(depth_kernel, 2, 0)

    def forward_plane(pair):
        return conv_plane(pair[0].astype(jnp.float32), pair[1]).astype(jnp.bfloat16)
    conv_out = lax.map(forward_plane, (masked, kernels))
    lat_ids = lax.broadcasted_iota(jnp.int32, swath_offset.shape, 0)
    lon_ids = lax.broadcasted_iota(jnp.int32, swath_offset.shape, 1)
    row_ids = (lat_ids * ROWS + swath_offset // COLS).reshape(-1)
    col_ids = (lon_ids * COLS + swath_offset % COLS).reshape(-1)
    swath = jnp.zeros((GRID_ROWS, GRID_COLUMNS), jnp.float32).at[row_ids, col_ids].add(swath_value.reshape(-1))
    cotan = out_grad.astype(jnp.float32).at[0].add(swath)
    cotan = (cotan * mask_float[None]).astype(jnp.bfloat16)
    block_count = GRID_ROWS // 2
    block_cells = 2 * GRID_COLUMNS
    conv_blocks = jnp.moveaxis(conv_out.reshape(C, block_count, block_cells), 1, 0)
    cotan_blocks = jnp.moveaxis(cotan.reshape(C, block_count, block_cells), 1, 0)
    group = HID // N_CH

    def step(carry, pair):
        conv_block, cotan_block = pair
        hidden = jnp.dot(expand_weight.T, conv_block, preferred_element_type=jnp.float32) + expand_bias[:, None]
        activ, gelu_back = jax.vjp(jax.nn.gelu, hidden)
        act_grad = jnp.dot(project_weight, cotan_block, preferred_element_type=jnp.float32)
        pre_grad = gelu_back(act_grad)[0].astype(jnp.bfloat16)
        expand_sum = carry[0] + jnp.dot(conv_block, pre_grad.T, preferred_element_type=jnp.float32)
        project_sum = carry[1] + jnp.dot(activ.astype(jnp.bfloat16), cotan_block.T, preferred_element_type=jnp.float32)
        bias_sum = carry[2] + lax.optimization_barrier(jnp.sum(pre_grad.astype(jnp.float32), axis=1))
        conv_grad = jnp.zeros((C, block_cells), jnp.float32)
        for group_index in range(N_CH):
            lower = group_index * group
            part = jnp.dot(expand_weight[:, lower:lower + group], pre_grad[lower:lower + group], preferred_element_type=jnp.float32)
            conv_grad = conv_grad + lax.optimization_barrier(part.astype(jnp.bfloat16)).astype(jnp.float32)
        return ((expand_sum, project_sum, bias_sum), conv_grad.astype(jnp.bfloat16))
    start = (jnp.zeros((C, HID), jnp.float32), jnp.zeros((HID, C), jnp.float32), jnp.zeros((HID,), jnp.float32))
    sums, grad_blocks = lax.scan(step, start, (conv_blocks, cotan_blocks))
    conv_grad = jnp.moveaxis(grad_blocks, 0, 1).reshape(C, GRID_ROWS, GRID_COLUMNS)

    def adjoint(triple):
        ocean_field, taps, grad = triple
        unused, back = jax.vjp(conv_plane, ocean_field, taps)
        return back(grad)
    state_back, kernel_back = lax.map(adjoint, (masked.astype(jnp.float32), kernels, conv_grad.astype(jnp.float32)))
    state_grad = (mask_float[None] * (cotan.astype(jnp.float32) + state_back)).astype(jnp.bfloat16)
    scale = float(GRID_ROWS * GRID_COLUMNS) ** (-0.5)
    return (state_grad, sums[0] * scale, sums[1] * scale, sums[2] * scale, jnp.moveaxis(kernel_back, 0, 2) * scale)
```

```python
import math

import jax
import jax.numpy as jnp
from jax import lax
from jax.experimental import pallas as pl
from jax.experimental.pallas import tpu as pltpu
from jax.sharding import PartitionSpec as P

DILATION_STEP = 2


MESH = pl.DeviceIdType.MESH


def ring(count):
    forward = [(i, (i + 1) % count) for i in range(count)]
    return forward, [(target, source) for source, target in forward]


def extend(ocean_field):
    rows = ocean_field.shape[1]
    n_lon = lax.axis_size("lon")
    n_lat = lax.axis_size("lat")
    east, west = ring(n_lon)
    low = lax.ppermute(ocean_field[:, :, -DILATION_STEP:], "lon", east)
    high = lax.ppermute(ocean_field[:, :, :DILATION_STEP], "lon", west)
    wide = jnp.concatenate([low, ocean_field, high], axis=2)
    top_rows = wide[:, rows - DILATION_STEP :, :]
    southern = lax.ppermute(
        top_rows,
        ("lon", "lat"),
        [
            (j * n_lat + i, j * n_lat + i + 1)
            for i in range(n_lat - 1)
            for j in range(n_lon)
        ],
    )
    at_top = lax.axis_index("lat") == n_lat - 1
    low_rows = wide[:, :DILATION_STEP, :]
    northern = lax.ppermute(
        low_rows,
        ("lon", "lat"),
        [
            (j * n_lat + i + 1, j * n_lat + i)
            for i in range(n_lat - 1)
            for j in range(n_lon)
        ],
    )
    mirrored = lax.ppermute(
        top_rows[:, ::-1, ::-1],
        ("lon", "lat"),
        [((n_lon - 1 - j) * n_lat + n_lat - 1, j * n_lat + n_lat - 1) for j in range(n_lon)],
    )
    northern = jnp.where(at_top, mirrored, northern)
    return jnp.concatenate([southern, wide, northern], axis=1)


def sum_kernel(first, second, rest, first_out, second_out, rest_out, pad, tiles, whole, lat_in, part, lon_in,
               send_a, recv_a, send_b, recv_b, send_c, recv_c, send_d, recv_d):
    n_lat, n_lon = lat_in.shape[0], lon_in.shape[0]
    lat, lon = lax.axis_index("lat"), lax.axis_index("lon")
    height, width = first.shape
    down, across = pad.shape[1] // 8, pad.shape[2] // 128

    def lat_peer(step):
        return {"lat": lax.rem(lat + step, n_lat)}

    def lon_peer(step):
        return {"lon": lax.rem(lon + step, n_lon)}

    barrier = pltpu.get_barrier_semaphore()
    for step in range(1, n_lat):
        pl.semaphore_signal(barrier, inc=1, device_id=lat_peer(step), device_id_type=MESH)
    for step in range(1, n_lon):
        pl.semaphore_signal(barrier, inc=1, device_id=lon_peer(step), device_id_type=MESH)

    pad[...] = jnp.zeros_like(pad)
    tiles[...] = jnp.zeros_like(tiles)
    pad[0, :height, :width] = first[...]
    pad[1, :height, :width] = second[...]
    spots = [(which, i, j) for which in range(2) for i in range(down) for j in range(across)]
    for place, (which, i, j) in enumerate(spots):
        tiles[place // n_lon, place % n_lon] = pad[which, 8 * i : 8 * i + 8, 128 * j : 128 * j + 128]
    last = len(spots)
    tiles[last // n_lon, last % n_lon] = rest[...]
    pl.semaphore_wait(barrier, n_lat + n_lon - 2)

    def exchange(copies):
        for copy in copies:
            copy.start()
        for copy in copies:
            copy.wait()

    exchange([
        pltpu.make_async_remote_copy(
            tiles.at[lax.rem(lat + step, n_lat)], lat_in.at[step], send_a.at[step], recv_a.at[step],
            device_id=lat_peer(step), device_id_type=MESH)
        for step in range(1, n_lat)
    ])
    total = tiles[lat]
    for step in range(1, n_lat):
        total = total + lat_in[step]
    part[...] = total
    exchange([
        pltpu.make_async_remote_copy(
            part.at[lax.rem(lon + step, n_lon)], lon_in.at[step], send_b.at[step], recv_b.at[step],
            device_id=lon_peer(step), device_id_type=MESH)
        for step in range(1, n_lon)
    ])
    total = part[lon]
    for step in range(1, n_lon):
        total = total + lon_in[step]
    whole[lat, lon] = total
    exchange([
        pltpu.make_async_remote_copy(
            whole.at[lat, lon], whole.at[lat, lon], send_c.at[step], recv_c.at[step],
            device_id=lon_peer(step), device_id_type=MESH)
        for step in range(1, n_lon)
    ])
    exchange([
        pltpu.make_async_remote_copy(
            whole.at[lat], whole.at[lat], send_d.at[step], recv_d.at[step],
            device_id=lat_peer(step), device_id_type=MESH)
        for step in range(1, n_lat)
    ])
    for place, (which, i, j) in enumerate(spots):
        pad[which, 8 * i : 8 * i + 8, 128 * j : 128 * j + 128] = whole[place // n_lon, place % n_lon]
    first_out[...] = pad[0, :height, :width]
    second_out[...] = pad[1, :height, :width]
    rest_out[...] = whole[last // n_lon, last % n_lon]


def sum_over_cells(first, second, rest):
    n_lat, n_lon = lax.axis_size("lat"), lax.axis_size("lon")
    height, width = first.shape
    down, across = -(-height // 8), -(-width // 128)
    vmem = pl.BlockSpec(memory_space=pltpu.VMEM)
    tile = (8, 128)
    shapes = [jax.ShapeDtypeStruct(x.shape, x.dtype) for x in (first, second, rest)]
    return pl.pallas_call(
        sum_kernel,
        out_shape=shapes,
        in_specs=[vmem] * 3,
        out_specs=[vmem] * 3,
        scratch_shapes=[
            pltpu.VMEM((2, 8 * down, 128 * across), jnp.float32),
            pltpu.VMEM((n_lat, n_lon) + tile, jnp.float32),
            pltpu.VMEM((n_lat, n_lon) + tile, jnp.float32),
            pltpu.VMEM((n_lat, n_lon) + tile, jnp.float32),
            pltpu.VMEM((n_lon,) + tile, jnp.float32),
            pltpu.VMEM((n_lon,) + tile, jnp.float32),
        ]
        + [pltpu.SemaphoreType.DMA((n,)) for n in (n_lat, n_lat, n_lon, n_lon, n_lon, n_lon, n_lat, n_lat)],
        compiler_params=pltpu.CompilerParams(collective_id=0, has_side_effects=True),
    )(first, second, rest)


def on_device(
    ocean_state,
    land_mask,
    out_grad,
    swath_offset,
    swath_value,
    depth_kernel,
    expand_weight,
    expand_bias,
    project_weight,
):
    channels_per_shard = ocean_state.shape[0]
    count_of_rows = ocean_state.shape[1]
    column_count = ocean_state.shape[2]
    cells = count_of_rows * column_count
    scale = 1.0 / math.sqrt(
        count_of_rows * lax.axis_size("lat") * column_count * lax.axis_size("lon")
    )
    mask_float = land_mask.astype(jnp.float32)[None]
    masked = ocean_state * land_mask.astype(jnp.bfloat16)[None]
    state_pad = extend(masked)
    forward = jnp.zeros((channels_per_shard, count_of_rows, column_count), jnp.float32)
    for row_offset in range(3):
        for column_offset in range(3):
            kernel_window = state_pad[
                :,
                DILATION_STEP * row_offset : DILATION_STEP * row_offset + count_of_rows,
                DILATION_STEP * column_offset : DILATION_STEP * column_offset + column_count,
            ]
            forward = forward + depth_kernel[row_offset, column_offset][
                :, None, None
            ] * kernel_window.astype(jnp.float32)
    conv_out = forward.astype(jnp.bfloat16)
    swath = (
        jnp.zeros((cells,), jnp.float32).at[swath_offset.reshape(-1)].add(swath_value.reshape(-1))
    )
    first_group = jnp.where(lax.axis_index("ch") == 0, 1.0, 0.0).astype(jnp.float32)
    cotan = (
        out_grad.astype(jnp.float32)
        .at[0]
        .add(first_group * swath.reshape(count_of_rows, column_count))
    )
    cotan = (cotan * mask_float).astype(jnp.bfloat16)
    conv_all, cotan_all = (
        lax.all_gather(conv_out, "ch", axis=0, tiled=True),
        lax.all_gather(cotan, "ch", axis=0, tiled=True),
    )
    conv_flat = conv_all.reshape(conv_all.shape[0], cells)
    cotan_flat = cotan_all.reshape(cotan_all.shape[0], cells)
    hidden = (
        jnp.dot(expand_weight.T, conv_flat, preferred_element_type=jnp.float32)
        + expand_bias[:, None]
    )
    activ, gelu_back = jax.vjp(jax.nn.gelu, hidden)
    act_grad = jnp.dot(project_weight, cotan_flat, preferred_element_type=jnp.float32)
    pre_grad = gelu_back(act_grad)[0].astype(jnp.bfloat16)
    project_part = (
        jnp.dot(activ.astype(jnp.bfloat16), cotan_flat.T, preferred_element_type=jnp.float32)
        * scale
    )
    expand_part = jnp.dot(pre_grad, conv_flat.T, preferred_element_type=jnp.float32) * scale
    bias_part = jnp.sum(pre_grad.astype(jnp.float32), axis=1) * scale
    summed = lax.psum_scatter(
        jnp.dot(expand_weight, pre_grad, preferred_element_type=jnp.float32).astype(jnp.bfloat16),
        "ch",
        scatter_dimension=0,
        tiled=True,
    )
    conv_grad = summed.reshape(channels_per_shard, count_of_rows, column_count)
    grad_pad = extend(conv_grad)
    grad_float = conv_grad.astype(jnp.float32)
    kernel_rows = []
    swapped_axes = jnp.zeros((channels_per_shard, count_of_rows, column_count), jnp.float32)
    for row_offset in range(3):
        kernel_cols = []
        for column_offset in range(3):
            kernel_window = state_pad[
                :,
                DILATION_STEP * row_offset : DILATION_STEP * row_offset + count_of_rows,
                DILATION_STEP * column_offset : DILATION_STEP * column_offset + column_count,
            ]
            kernel_cols.append(jnp.sum(grad_float * kernel_window.astype(jnp.float32), axis=(1, 2)))
            reverse_row = DILATION_STEP * (2 - row_offset)
            reverse_column = DILATION_STEP * (2 - column_offset)
            back_window = grad_pad[
                :,
                reverse_row : reverse_row + count_of_rows,
                reverse_column : reverse_column + column_count,
            ]
            swapped_axes = swapped_axes + depth_kernel[row_offset, column_offset][
                :, None, None
            ] * back_window.astype(jnp.float32)
        kernel_rows.append(jnp.stack(kernel_cols, axis=0))
    kernel_part = jnp.stack(kernel_rows, axis=0) * scale
    fold_adjustment = jnp.zeros((channels_per_shard, DILATION_STEP, column_count), jnp.float32)
    for column_offset in range(3):
        reverse_column = DILATION_STEP * (2 - column_offset)
        rim_window = grad_pad[
            :,
            count_of_rows + DILATION_STEP : count_of_rows + 2 * DILATION_STEP,
            reverse_column : reverse_column + column_count,
        ]
        weight_change = depth_kernel[2, 2 - column_offset] - depth_kernel[0, column_offset]
        fold_adjustment = fold_adjustment + weight_change[:, None, None] * rim_window.astype(
            jnp.float32
        )
    at_top = lax.axis_index("lat") == lax.axis_size("lat") - 1
    swapped_axes = swapped_axes.at[:, count_of_rows - DILATION_STEP :, :].add(
        jnp.where(at_top, fold_adjustment, jnp.zeros_like(fold_adjustment))
    )
    state_grad = (mask_float * (cotan.astype(jnp.float32) + swapped_axes)).astype(jnp.bfloat16)
    rest = jnp.concatenate([bias_part, kernel_part.reshape(-1)])
    count = rest.shape[0]
    rest = jnp.pad(rest, (0, 1024 - count)).reshape(8, 128)
    expand_sum, project_grad, rest = sum_over_cells(expand_part, project_part, rest)
    rest = rest.reshape(-1)
    bias_grad = rest[: bias_part.shape[0]]
    kernel_grad = rest[bias_part.shape[0] : count].reshape(kernel_part.shape)
    expand_grad = expand_sum.T
    return (state_grad, expand_grad, project_grad, bias_grad, kernel_grad)


def solution(mesh):
    return jax.shard_map(
        on_device,
        mesh=mesh,
        in_specs=(
            P("ch", "lat", "lon"),
            P("lat", "lon"),
            P("ch", "lat", "lon"),
            P("lat", "lon", None),
            P("lat", "lon", None),
            P(None, None, "ch"),
            P(None, "ch"),
            P("ch"),
            P("ch", None),
        ),
        out_specs=(
            P("ch", "lat", "lon"),
            P(None, "ch"),
            P("ch", None),
            P("ch"),
            P(None, None, "ch"),
        ),
        check_vma=False,
    )
```

```python
import functools
import math

import jax
import jax.numpy as jnp
from jax import lax
from jax.experimental import pallas as pl
from jax.experimental.pallas import tpu as pltpu
from jax.sharding import PartitionSpec as P

MESH = pl.DeviceIdType.MESH
ROWS = 32
WIDE = 80
LANES = 128
SHARE = 8
UNITS = 160
TILES = 114
REST = 10
BF = jnp.bfloat16
F32 = jnp.float32


def rcopy(src, dst, send, recv, **where):
    return pltpu.make_async_remote_copy(
        src, dst, send, recv, device_id=where, device_id_type=MESH
    )


def three_parts(x):
    high = x.astype(BF)
    left = x - high.astype(F32)
    middle = left.astype(BF)
    low = (left - middle.astype(F32)).astype(BF)
    return high, middle, low


def step_kernel(
    scale, n_lon, n_lat,
    state, grad, mask, offset, value, taps, weights,
    state_out, project_out, expand_out, bias_out, kernel_out,
    fwin, gwin, kb, swath, cotan, conv, cot_all, conv_all, w_all,
    pack_out, pack_in, side, msg_out, msg_in,
    acc_p, acc_e, cg_out, cg_in, tiles, pair_in, cross_in,
    whole, lat_in, part, lon_in, pad,
    es, er, ms, mr, ws, wr, cs, cr, vs, vr, gs, gr, ps, pr, xs, xr,
    send_a, recv_a, send_b, recv_b, send_c, recv_c, send_d, recv_d,
):
    lon, lat, ch = lax.axis_index("lon"), lax.axis_index("lat"), lax.axis_index("ch")
    top = lat == n_lat - 1
    mate = ch + 1 - 2 * lax.rem(ch, 2)
    across = lax.rem(ch + 2, 4)
    mate_across = lax.rem(mate + 2, 4)
    lane = lax.broadcasted_iota(jnp.int32, (WIDE, LANES), 1)

    def lat_peer(step):
        return lax.rem(lat + step, n_lat)

    def lon_peer(step):
        return lax.rem(lon + step, n_lon)

    barrier = pltpu.get_barrier_semaphore()
    for step in range(1, n_lat):
        pl.semaphore_signal(barrier, inc=1, device_id={"lat": lat_peer(step)}, device_id_type=MESH)
    for step in range(1, n_lon):
        pl.semaphore_signal(barrier, inc=1, device_id={"lon": lon_peer(step)}, device_id_type=MESH)
    for step in range(1, 4):
        pl.semaphore_signal(
            barrier, inc=1, device_id={"ch": lax.rem(ch + step, 4)}, device_id_type=MESH
        )

    def pack_edges(use, win):
        def body(r, acc):
            return jnp.where(lane // 4 == r, pltpu.roll(win[1, 2 + r], lax.rem(4 * r + 2, LANES), 1), acc)

        pack_out[use] = lax.fori_loop(0, ROWS, body, jnp.zeros((WIDE, LANES), F32)).astype(BF)

    def edge_copies(use):
        return [
            rcopy(pack_out.at[use], pack_in.at[use, 0], es.at[use, 0], er.at[use, 0], lon=lon_peer(1)),
            rcopy(pack_out.at[use], pack_in.at[use, 1], es.at[use, 1], er.at[use, 1], lon=lon_peer(n_lon - 1)),
        ]

    def send_edges(use):
        for copy in edge_copies(use):
            copy.start()

    def wait_edges(use):
        for copy in edge_copies(use):
            copy.wait()
        side[use] = jnp.where(
            lax.rem(lane, 4) < 2, pack_in[use, 0].astype(F32), pack_in[use, 1].astype(F32)
        )

    north_lat = jnp.minimum(lat + 1, n_lat - 1)
    north_lon = jnp.where(top, n_lon - 1 - lon, lon)
    north_slot = jnp.where(top, 1, 0)
    south_lat = jnp.maximum(lat - 1, 0)

    def north_copy(use):
        return rcopy(
            msg_out.at[use, 1], msg_in.at[use, north_slot], ms.at[use, 1], mr.at[use, north_slot],
            lat=north_lat, lon=north_lon,
        )

    def south_copy(use):
        return rcopy(
            msg_out.at[use, 0], msg_in.at[use, 1], ms.at[use, 0], mr.at[use, 1], lat=south_lat
        )

    def send_rows(use, win):
        edge = side[use]
        msg_out[use, 0, 0] = win[1, 2].astype(BF)
        msg_out[use, 0, 1] = win[1, 3].astype(BF)
        msg_out[use, 0, 2] = edge.astype(BF)

        @pl.when(lat > 0)
        def _():
            south_copy(use).start()

        @pl.when(jnp.logical_not(top))
        def _():
            msg_out[use, 1, 0] = win[1, ROWS].astype(BF)
            msg_out[use, 1, 1] = win[1, ROWS + 1].astype(BF)
            msg_out[use, 1, 2] = edge.astype(BF)

        @pl.when(top)
        def _():
            square = (LANES, LANES)
            turn = (
                lax.broadcasted_iota(jnp.int32, square, 0) + lax.broadcasted_iota(jnp.int32, square, 1)
                == LANES - 1
            ).astype(F32).astype(BF)
            for place, row in enumerate((win[1, ROWS + 1], win[1, ROWS], edge)):
                msg_out[use, 1, place] = jnp.dot(
                    row.astype(BF), turn, preferred_element_type=F32
                ).astype(BF)

        north_copy(use).start()

    def windows(win, p, quad, edge):
        x = win[1, p]
        win[0, p] = jnp.where(lane < 2, pltpu.roll(edge, lax.rem(LANES - 4 * quad, LANES), 1), pltpu.roll(x, 2, 1))
        win[2, p] = jnp.where(
            lane >= LANES - 2,
            pltpu.roll(edge, lax.rem(2 * LANES - 4 - 4 * quad, LANES), 1),
            pltpu.roll(x, LANES - 2, 1),
        )

    def inner_windows(use, win):
        edge = side[use]

        def body(r, unused):
            windows(win, r + 2, r, edge)
            return unused

        lax.fori_loop(0, ROWS, body, 0)

    def wait_rows(use, win):
        @pl.when(lat > 0)
        def _():
            south_copy(use).wait_send()
            rcopy(
                msg_out.at[use, 1], msg_in.at[use, 0], ms.at[use, 1], mr.at[use, 0], lat=south_lat
            ).wait_recv()

        @pl.when(lat == 0)
        def _():
            msg_in[use, 0] = jnp.zeros((3, WIDE, LANES), BF)

        north_copy(use).wait_send()
        rcopy(
            msg_out.at[use, 0], msg_in.at[use, 1], ms.at[use, 0], mr.at[use, 1],
            lat=north_lat, lon=north_lon,
        ).wait_recv()
        for slot, first, quad in ((0, 0, ROWS - 2), (1, ROWS + 2, 0)):
            edge = msg_in[use, slot, 2].astype(F32)
            for t in range(2):
                win[1, first + t] = msg_in[use, slot, t].astype(F32)
                windows(win, first + t, quad + t, edge)

    def scatter(q, src, dst, send, recv):
        @pl.when(ch != q)
        def _():
            rcopy(src, dst, send, recv, ch=jnp.int32(q)).start()

        @pl.when(ch == q)
        def _():
            dst[...] = src[...]

    def settle(q, src, dst, send, recv):
        @pl.when(ch != q)
        def _():
            rcopy(src, dst, send, recv, ch=jnp.int32(q)).wait()

    def masked_rows(r, unused):
        fwin[1, 2 + r] = state[r].astype(F32) * mask[pl.ds(r, 1), :]
        return unused

    lax.fori_loop(0, ROWS, masked_rows, 0)
    pack_edges(0, fwin)
    pl.semaphore_wait(barrier, n_lat + n_lon + 1)
    send_edges(0)

    w_all[ch] = weights[...]
    to_mate = rcopy(weights, w_all.at[ch], ws.at[0], wr.at[0], ch=mate)
    to_across = rcopy(weights, w_all.at[ch], ws.at[1], wr.at[1], ch=across)
    passed = rcopy(w_all.at[across], w_all.at[across], ws.at[2], wr.at[2], ch=mate)
    to_across.start()
    to_mate.start()

    spot = offset[...]
    points = spot.shape[1]
    at_row = (
        lax.broadcasted_iota(jnp.int32, (ROWS, points), 0) == spot // LANES
    ).astype(F32).astype(BF)
    at_col = lax.broadcasted_iota(jnp.int32, (LANES, points), 0) == lax.rem(spot, LANES)
    spread = jnp.where(at_col, value[...], 0.0)
    total = jnp.zeros((ROWS, LANES), F32)
    for piece in three_parts(spread):
        total = total + lax.dot_general(
            at_row, piece, (((1,), (1,)), ((), ())), preferred_element_type=F32
        )
    swath[...] = total * jnp.where(ch == 0, 1.0, 0.0)

    first_channel = lax.broadcasted_iota(jnp.int32, (WIDE, LANES), 0) == 0

    def cotan_rows(r, unused):
        row = grad[r].astype(F32)
        row = row + jnp.where(first_channel, swath[pl.ds(r, 1), :], 0.0)
        cotan[r] = (row * mask[pl.ds(r, 1), :]).astype(BF)
        return unused

    lax.fori_loop(0, ROWS, cotan_rows, 0)
    for q in range(4):
        scatter(q, cotan.at[pl.ds(SHARE * q, SHARE)], cot_all.at[ch], cs.at[q], cr.at[ch])
    for t in range(9):
        kb[t] = jnp.broadcast_to(taps[:, t : t + 1], (WIDE, LANES))

    wait_edges(0)
    send_rows(0, fwin)
    inner_windows(0, fwin)

    def conv_rows(low, high):
        for g in range(WIDE // 16):
            span = slice(16 * g, 16 * g + 16)
            ks = [kb[t, span, :] for t in range(9)]

            def body(r, unused):
                acc = ks[0] * fwin[0, r, span, :]
                for t in range(1, 9):
                    acc = acc + ks[t] * fwin[t % 3, r + 2 * (t // 3), span, :]
                if g == WIDE // 16 - 1:
                    unit = lax.broadcasted_iota(jnp.int32, (16, LANES), 0) + 16 * g
                    acc = jnp.where(unit >= 75, 1.0, acc)
                conv[r, span, :] = acc.astype(BF)
                return unused

            lax.fori_loop(low, high, body, 0)

    def send_conv(q):
        scatter(q, conv.at[pl.ds(SHARE * q, SHARE)], conv_all.at[ch], vs.at[q], vr.at[ch])

    conv_rows(SHARE, 3 * SHARE)
    send_conv(1)
    send_conv(2)
    wait_rows(0, fwin)
    conv_rows(0, SHARE)
    send_conv(0)
    conv_rows(3 * SHARE, 4 * SHARE)
    send_conv(3)

    to_across.wait()
    passed.start()
    to_mate.wait()
    acc_p[...] = jnp.zeros_like(acc_p)
    acc_e[...] = jnp.zeros_like(acc_e)
    rcopy(w_all.at[mate_across], w_all.at[mate_across], ws.at[2], wr.at[2], ch=mate).wait()
    for q in range(4):
        settle(q, cotan.at[pl.ds(SHARE * q, SHARE)], cot_all.at[q], cs.at[q], cr.at[q])
    for q in range(4):
        settle(q, conv.at[pl.ds(SHARE * q, SHARE)], conv_all.at[q], vs.at[q], vr.at[q])

    c0 = math.sqrt(2.0 / math.pi)

    def back_part(c, q):
        return cg_out.at[q, pl.ds(2 * c, 2)]

    def cells(c, unused):
        def both(ref):
            return jnp.concatenate(
                [
                    jnp.concatenate([ref[s, 2 * c + t] for s in range(4)], axis=0)
                    for t in range(2)
                ],
                axis=1,
            )

        x, y = both(conv_all), both(cot_all)
        w1 = w_all[:, 0].reshape(4 * UNITS, 4 * WIDE)
        w2 = w_all[:, 1].reshape(4 * UNITS, 4 * WIDE)
        h = jnp.dot(w1, x, preferred_element_type=F32)
        a = jnp.dot(w2, y, preferred_element_type=F32)
        square = h * h
        t = jnp.tanh(h * (c0 + (c0 * 0.044715) * square))
        half = 0.5 * t + 0.5
        activ = (h * half).astype(BF)
        slope = half + (0.5 * h) * (1.0 - t * t) * (c0 + (3.0 * c0 * 0.044715) * square)
        pre = (a * slope).astype(BF)
        acc_p[...] += lax.dot_general(activ, y, (((1,), (1,)), ((), ())), preferred_element_type=F32)
        acc_e[...] += lax.dot_general(pre, x, (((1,), (1,)), ((), ())), preferred_element_type=F32)
        back = lax.dot_general(w1, pre, (((0,), (0,)), ((), ())), preferred_element_type=F32).astype(BF)
        for q in range(4):
            for t in range(2):
                cg_out[q, 2 * c + t] = back[WIDE * q : WIDE * q + WIDE, LANES * t : LANES * t + LANES]
        for q in range(4):
            scatter(
                q, back_part(c, q), cg_in.at[pl.ds(SHARE * ch + 2 * c, 2)], gs.at[c, q], gr.at[c, ch]
            )
        return unused

    lax.fori_loop(0, SHARE // 2, cells, 0)

    for q in range(4):
        for which, ref in enumerate((acc_p, acc_e)):

            def body(d, unused):
                start = pl.multiple_of(UNITS * q + 8 * d, 8)
                for j in range(3):
                    width = min(LANES, 4 * WIDE - LANES * j)
                    tiles[q, 57 * which + 3 * d + j, :, :width] = ref[pl.ds(start, 8), LANES * j : LANES * j + width]
                    if width < LANES:
                        tiles[q, 57 * which + 3 * d + j, :, width:] = jnp.zeros((8, LANES - width), F32)
                return unused

            lax.fori_loop(0, 19, body, 0)

    used = pl.ds(0, TILES)
    pair = [
        rcopy(tiles.at[mate_across, used], pair_in.at[1], ps.at[1], pr.at[1], ch=mate),
        rcopy(tiles.at[mate, used], pair_in.at[0], ps.at[0], pr.at[0], ch=mate),
    ]
    for copy in pair:
        copy.start()

    for q in range(4):

        def body(c, unused):
            settle(q, back_part(c, q), cg_in.at[pl.ds(SHARE * q + 2 * c, 2)], gs.at[c, q], gr.at[c, q])
            return unused

        lax.fori_loop(0, SHARE // 2, body, 0)

    def grad_rows(r, unused):
        gwin[1, 2 + r] = cg_in[r].astype(F32)
        return unused

    lax.fori_loop(0, ROWS, grad_rows, 0)
    pack_edges(1, gwin)
    send_edges(1)

    def add_tiles(slot, ref):
        def body(d, unused):
            tiles[slot, pl.ds(6 * d, 6)] = tiles[slot, pl.ds(6 * d, 6)] + ref[pl.ds(6 * d, 6)]
            return unused

        lax.fori_loop(0, TILES // 6, body, 0)

    pair[0].wait()
    add_tiles(across, pair_in.at[1])
    cross = rcopy(tiles.at[across, used], cross_in, xs, xr, ch=across)
    cross.start()
    pair[1].wait()
    add_tiles(ch, pair_in.at[0])

    for g in range(REST):
        span = slice(8 * g, 8 * g + 8)

        def body(r, sums):
            now = gwin[1, 2 + r, span, :]
            return tuple(
                sums[t] + now * fwin[t % 3, r + 2 * (t // 3), span, :] for t in range(9)
            )

        sums = lax.fori_loop(0, ROWS, body, tuple(jnp.zeros((8, LANES), F32) for _ in range(9)))
        spots = lax.broadcasted_iota(jnp.int32, (8, LANES), 1)
        kept = jnp.zeros((8, LANES), F32)
        for t in range(9):
            kept = jnp.where(spots == t, jnp.sum(sums[t], axis=1, keepdims=True), kept)
        tiles[ch, TILES + g] = kept
    for g in range(TILES + REST, n_lat * n_lon):
        tiles[ch, g] = jnp.zeros((8, LANES), F32)

    wait_edges(1)
    send_rows(1, gwin)
    cross.wait()
    add_tiles(ch, cross_in)

    def lat_copies():
        return [
            rcopy(tiles.at[ch, pl.ds(n_lon * lat_peer(s), n_lon)], lat_in.at[s], send_a.at[s], recv_a.at[s], lat=lat_peer(s))
            for s in range(1, n_lat)
        ]

    for copy in lat_copies():
        copy.start()

    inner_windows(1, gwin)
    for copy in lat_copies():
        copy.wait()
    total = tiles[ch, pl.ds(n_lon * lat, n_lon)]
    for s in range(1, n_lat):
        total = total + lat_in[s]
    part[...] = total

    def lon_copies():
        return [
            rcopy(part.at[lon_peer(s)], lon_in.at[s], send_b.at[s], recv_b.at[s], lon=lon_peer(s))
            for s in range(1, n_lon)
        ]

    for copy in lon_copies():
        copy.start()

    wait_rows(1, gwin)

    def adjoint_rows(low, high, rim):
        for g in range(WIDE // 16):
            span = slice(16 * g, 16 * g + 16)
            ks = [kb[8 - t, span, :] for t in range(9)]
            if rim:
                for b in range(3):
                    ks[6 + b] = jnp.where(top, kb[6 + b, span, :], ks[6 + b])

            def body(r, unused):
                acc = cotan[r, span, :].astype(F32)
                for t in range(9):
                    acc = acc + ks[t] * gwin[t % 3, r + 2 * (t // 3), span, :]
                state_out[r, span, :] = (acc * mask[pl.ds(r, 1), :]).astype(BF)
                return unused

            lax.fori_loop(low, high, body, 0)

    adjoint_rows(0, ROWS // 2, False)
    for copy in lon_copies():
        copy.wait()
    total = part[lon]
    for s in range(1, n_lon):
        total = total + lon_in[s]
    mine = n_lon * lat + lon
    whole[mine] = total * scale

    def share_lon():
        return [
            rcopy(whole.at[mine], whole.at[mine], send_c.at[s], recv_c.at[s], lon=lon_peer(s))
            for s in range(1, n_lon)
        ]

    for copy in share_lon():
        copy.start()
    adjoint_rows(ROWS // 2, ROWS - 2, False)
    adjoint_rows(ROWS - 2, ROWS, True)
    for s in range(1, n_lon):
        source = n_lon * lat + lon_peer(n_lon - s)
        rcopy(whole.at[source], whole.at[source], send_c.at[s], recv_c.at[s], lon=lon_peer(s)).wait()
    band = pl.ds(n_lon * lat, n_lon)
    for s in range(1, n_lat):
        rcopy(whole.at[band], whole.at[band], send_d.at[s], recv_d.at[s], lat=lat_peer(s)).start()
    for s in range(1, n_lat):
        source = pl.ds(n_lon * lat_peer(n_lat - s), n_lon)
        rcopy(whole.at[source], whole.at[source], send_d.at[s], recv_d.at[s], lat=lat_peer(s)).wait()

    def unpack(d, unused):
        start = pl.multiple_of(8 * d, 8)
        for which in range(2):
            for j in range(3):
                pad[which, pl.ds(start, 8), LANES * j : LANES * j + LANES] = whole[57 * which + 3 * d + j]
        return unused

    lax.fori_loop(0, 19, unpack, 0)
    for q in range(4):
        project_out[:, 75 * q : 75 * q + 75] = pad[0, :150, WIDE * q : WIDE * q + 75]
        expand_out[:, 75 * q : 75 * q + 75] = pad[1, :150, WIDE * q : WIDE * q + 75]
    bias_out[...] = pad[1, :, :LANES]
    for g in range(REST):
        kernel_out[8 * g : 8 * g + 8, :] = whole[TILES + g]


def on_device(
    ocean_state, land_mask, out_grad, swath_offset, swath_value,
    depth_kernel, expand_weight, expand_bias, project_weight,
):
    n_lon, n_lat = lax.axis_size("lon"), lax.axis_size("lat")
    channels = ocean_state.shape[0]
    units = expand_bias.shape[0]
    scale = 1.0 / math.sqrt(ROWS * n_lat * LANES * n_lon)
    extra = WIDE - channels

    def by_rows(x):
        return jnp.pad(jnp.transpose(x, (1, 0, 2)), ((0, 0), (0, extra), (0, 0)))

    taps = jnp.pad(depth_kernel.reshape(9, channels).T, ((0, extra), (0, LANES - 9)))

    def spread(w):
        w = w.reshape(units, 4, channels)
        return jnp.pad(w, ((0, UNITS - units), (0, 0), (0, extra)))

    high = lax.reduce_precision(expand_bias, 8, 7)
    middle = lax.reduce_precision(expand_bias - high, 8, 7)
    low = expand_bias - high - middle
    bias = jnp.stack([high, middle, low], axis=1).astype(BF)
    first = spread(expand_weight.T)
    bias = jnp.pad(bias[:, None, :], ((0, UNITS - units), (0, 3), (channels, extra - 3)))
    first = first + bias
    weights = jnp.stack([first, spread(project_weight)]).reshape(2, UNITS, 4 * WIDE)

    vmem = pl.BlockSpec(memory_space=pltpu.VMEM)
    block = (ROWS, WIDE, LANES)
    all_block = (4, SHARE, WIDE, LANES)
    tile = (8, LANES)
    dma = pltpu.SemaphoreType.DMA
    state, project, expand, bias_grad, kernel_grad = pl.pallas_call(
        functools.partial(step_kernel, scale, n_lon, n_lat),
        out_shape=[
            jax.ShapeDtypeStruct(block, BF),
            jax.ShapeDtypeStruct((units, 4 * channels), F32),
            jax.ShapeDtypeStruct((units, 4 * channels), F32),
            jax.ShapeDtypeStruct((152, LANES), F32),
            jax.ShapeDtypeStruct((WIDE, LANES), F32),
        ],
        in_specs=[vmem] * 7,
        out_specs=[vmem] * 5,
        scratch_shapes=[
            pltpu.VMEM((3, ROWS + 4, WIDE, LANES), F32),
            pltpu.VMEM((3, ROWS + 4, WIDE, LANES), F32),
            pltpu.VMEM((9, WIDE, LANES), F32),
            pltpu.VMEM((ROWS, LANES), F32),
            pltpu.VMEM(block, BF),
            pltpu.VMEM(block, BF),
            pltpu.VMEM(all_block, BF),
            pltpu.VMEM(all_block, BF),
            pltpu.VMEM((4, 2, UNITS, 4 * WIDE), BF),
            pltpu.VMEM((2, WIDE, LANES), BF),
            pltpu.VMEM((2, 2, WIDE, LANES), BF),
            pltpu.VMEM((2, WIDE, LANES), F32),
            pltpu.VMEM((2, 2, 3, WIDE, LANES), BF),
            pltpu.VMEM((2, 2, 3, WIDE, LANES), BF),
            pltpu.VMEM((4 * UNITS, 4 * WIDE), F32),
            pltpu.VMEM((4 * UNITS, 4 * WIDE), F32),
            pltpu.VMEM(all_block, BF),
            pltpu.VMEM(block, BF),
            pltpu.VMEM((4, n_lat * n_lon) + tile, F32),
            pltpu.VMEM((2, TILES) + tile, F32),
            pltpu.VMEM((TILES,) + tile, F32),
            pltpu.VMEM((n_lat * n_lon,) + tile, F32),
            pltpu.VMEM((n_lat, n_lon) + tile, F32),
            pltpu.VMEM((n_lon,) + tile, F32),
            pltpu.VMEM((n_lon,) + tile, F32),
            pltpu.VMEM((2, 152, 3 * LANES), F32),
        ]
        + [dma((2, 2))] * 4
        + [dma((3,))] * 2
        + [dma((4,))] * 4
        + [dma((4, 4))] * 2
        + [dma((2,))] * 2
        + [dma(())] * 2
        + [dma((n_lat,))] * 2
        + [dma((n_lon,))] * 4
        + [dma((n_lat,))] * 2,
        compiler_params=pltpu.CompilerParams(
            collective_id=0, has_side_effects=True, vmem_limit_bytes=56 * 2**20
        ),
    )(
        by_rows(ocean_state),
        by_rows(out_grad),
        land_mask.astype(F32),
        swath_offset.reshape(1, -1),
        swath_value.reshape(1, -1),
        taps,
        weights,
    )
    return (
        jnp.transpose(state[:, :channels], (1, 0, 2)),
        expand.T,
        project,
        bias_grad[:units, channels],
        kernel_grad[:channels, :9].T.reshape(3, 3, channels),
    )


def solution(mesh):
    return jax.shard_map(
        on_device,
        mesh=mesh,
        in_specs=(
            P("ch", "lat", "lon"),
            P("lat", "lon"),
            P("ch", "lat", "lon"),
            P("lat", "lon", None),
            P("lat", "lon", None),
            P(None, None, "ch"),
            P(None, "ch"),
            P("ch"),
            P("ch", None),
        ),
        out_specs=(
            P("ch", "lat", "lon"),
            P(None, "ch"),
            P("ch", None),
            P("ch"),
            P(None, None, "ch"),
        ),
        check_vma=False,
    )
```

```python
import functools
import math

import jax
import jax.numpy as jnp
from jax import lax
from jax.experimental import pallas as pl
from jax.experimental.pallas import tpu as pltpu
from jax.sharding import PartitionSpec as P

MESH = pl.DeviceIdType.MESH
ROWS = 32
WIDE = 80
LANES = 128
SHARE = 8
UNITS = 160
TILES = 114
REST = 10
BF = jnp.bfloat16
F32 = jnp.float32


def rcopy(src, dst, send, recv, **where):
    return pltpu.make_async_remote_copy(
        src, dst, send, recv, device_id=where, device_id_type=MESH
    )


def rows_loop(low, high, body, width=4):
    def several(n, unused):
        for t in range(width):
            body(low + n * width + t)
        return unused

    lax.fori_loop(0, (high - low) // width, several, 0)


def three_parts(x):
    high = x.astype(BF)
    left = x - high.astype(F32)
    middle = left.astype(BF)
    low = (left - middle.astype(F32)).astype(BF)
    return high, middle, low


def step_kernel(
    scale, n_lon, n_lat,
    state, grad, mask, offset, value, taps, weights,
    state_out, project_out, expand_out, bias_out, kernel_out,
    fwin, gwin, kb, swath, cotan, conv, cot_all, conv_all, w_all,
    pack_out, pack_in, side, msg_out, msg_in,
    acc_p, acc_e, cg_out, cg_in, tiles, pair_in, cross_out, cross_in,
    narrow, lat_in, part, lon_in, band, whole, final, pad,
    es, er, ms, mr, ws, wr, cs, cr, vs, vr, gs, gr, ps, pr, xs, xr,
    send_a, recv_a, send_b, recv_b, send_c, recv_c, send_d, recv_d,
):
    lon, lat, ch = lax.axis_index("lon"), lax.axis_index("lat"), lax.axis_index("ch")
    top = lat == n_lat - 1
    mate = ch + 1 - 2 * lax.rem(ch, 2)
    across = lax.rem(ch + 2, 4)
    mate_across = lax.rem(mate + 2, 4)
    lane = lax.broadcasted_iota(jnp.int32, (WIDE, LANES), 1)

    def lat_peer(step):
        return lax.rem(lat + step, n_lat)

    def lon_peer(step):
        return lax.rem(lon + step, n_lon)

    barrier = pltpu.get_barrier_semaphore()
    for step in range(1, n_lat):
        pl.semaphore_signal(barrier, inc=1, device_id={"lat": lat_peer(step)}, device_id_type=MESH)
    for step in range(1, n_lon):
        pl.semaphore_signal(barrier, inc=1, device_id={"lon": lon_peer(step)}, device_id_type=MESH)
    for step in range(1, 4):
        pl.semaphore_signal(
            barrier, inc=1, device_id={"ch": lax.rem(ch + step, 4)}, device_id_type=MESH
        )

    def pack_edges(use, win):
        def body(r, acc):
            for t in range(4):
                row = 4 * r + t
                moved = pltpu.roll(win[1, 2 + row], lax.rem(4 * row + 2, LANES), 1)
                acc = jnp.where(lane // 4 == row, moved, acc)
            return acc

        pack_out[use] = lax.fori_loop(0, ROWS // 4, body, jnp.zeros((WIDE, LANES), F32)).astype(BF)

    def edge_copies(use):
        return [
            rcopy(pack_out.at[use], pack_in.at[use, 0], es.at[use, 0], er.at[use, 0], lon=lon_peer(1)),
            rcopy(pack_out.at[use], pack_in.at[use, 1], es.at[use, 1], er.at[use, 1], lon=lon_peer(n_lon - 1)),
        ]

    def send_edges(use):
        for copy in edge_copies(use):
            copy.start()

    def wait_edges(use):
        for copy in edge_copies(use):
            copy.wait()
        side[use] = jnp.where(
            lax.rem(lane, 4) < 2, pack_in[use, 0].astype(F32), pack_in[use, 1].astype(F32)
        )

    north_lat = jnp.minimum(lat + 1, n_lat - 1)
    north_lon = jnp.where(top, n_lon - 1 - lon, lon)
    north_slot = jnp.where(top, 1, 0)
    south_lat = jnp.maximum(lat - 1, 0)

    def north_copy(use):
        return rcopy(
            msg_out.at[use, 1], msg_in.at[use, north_slot], ms.at[use, 1], mr.at[use, north_slot],
            lat=north_lat, lon=north_lon,
        )

    def south_copy(use):
        return rcopy(
            msg_out.at[use, 0], msg_in.at[use, 1], ms.at[use, 0], mr.at[use, 1], lat=south_lat
        )

    def send_rows(use, win):
        edge = side[use]
        msg_out[use, 0, 0] = win[1, 2].astype(BF)
        msg_out[use, 0, 1] = win[1, 3].astype(BF)
        msg_out[use, 0, 2] = edge.astype(BF)

        @pl.when(lat > 0)
        def _():
            south_copy(use).start()

        @pl.when(jnp.logical_not(top))
        def _():
            msg_out[use, 1, 0] = win[1, ROWS].astype(BF)
            msg_out[use, 1, 1] = win[1, ROWS + 1].astype(BF)
            msg_out[use, 1, 2] = edge.astype(BF)

        @pl.when(top)
        def _():
            square = (LANES, LANES)
            turn = (
                lax.broadcasted_iota(jnp.int32, square, 0) + lax.broadcasted_iota(jnp.int32, square, 1)
                == LANES - 1
            ).astype(F32).astype(BF)
            for place, row in enumerate((win[1, ROWS + 1], win[1, ROWS], edge)):
                msg_out[use, 1, place] = jnp.dot(
                    row.astype(BF), turn, preferred_element_type=F32
                ).astype(BF)

        north_copy(use).start()

    def windows(win, p, quad, edge):
        x = win[1, p]
        win[0, p] = jnp.where(lane < 2, pltpu.roll(edge, lax.rem(LANES - 4 * quad, LANES), 1), pltpu.roll(x, 2, 1))
        win[2, p] = jnp.where(
            lane >= LANES - 2,
            pltpu.roll(edge, lax.rem(2 * LANES - 4 - 4 * quad, LANES), 1),
            pltpu.roll(x, LANES - 2, 1),
        )

    def inner_windows(use, win):
        edge = side[use]

        rows_loop(0, ROWS, lambda r: windows(win, r + 2, r, edge))

    def wait_rows(use, win):
        @pl.when(lat > 0)
        def _():
            south_copy(use).wait_send()
            rcopy(
                msg_out.at[use, 1], msg_in.at[use, 0], ms.at[use, 1], mr.at[use, 0], lat=south_lat
            ).wait_recv()

        @pl.when(lat == 0)
        def _():
            msg_in[use, 0] = jnp.zeros((3, WIDE, LANES), BF)

        north_copy(use).wait_send()
        rcopy(
            msg_out.at[use, 0], msg_in.at[use, 1], ms.at[use, 0], mr.at[use, 1],
            lat=north_lat, lon=north_lon,
        ).wait_recv()
        for slot, first, quad in ((0, 0, ROWS - 2), (1, ROWS + 2, 0)):
            edge = msg_in[use, slot, 2].astype(F32)
            for t in range(2):
                win[1, first + t] = msg_in[use, slot, t].astype(F32)
                windows(win, first + t, quad + t, edge)

    def scatter(q, src, dst, send, recv):
        @pl.when(ch != q)
        def _():
            rcopy(src, dst, send, recv, ch=jnp.int32(q)).start()

        @pl.when(ch == q)
        def _():
            dst[...] = src[...]

    def settle(q, src, dst, send, recv):
        @pl.when(ch != q)
        def _():
            rcopy(src, dst, send, recv, ch=jnp.int32(q)).wait()

    def masked_rows(r):
        fwin[1, 2 + r] = state[r].astype(F32) * mask[pl.ds(r, 1), :]

    rows_loop(0, ROWS, masked_rows)
    pack_edges(0, fwin)
    pl.semaphore_wait(barrier, n_lat + n_lon + 1)
    send_edges(0)

    w_all[ch] = weights[...]
    to_mate = rcopy(weights, w_all.at[ch], ws.at[0], wr.at[0], ch=mate)
    to_across = rcopy(weights, w_all.at[ch], ws.at[1], wr.at[1], ch=across)
    passed = rcopy(w_all.at[across], w_all.at[across], ws.at[2], wr.at[2], ch=mate)
    to_across.start()
    to_mate.start()

    spot = offset[...]
    points = spot.shape[1]
    at_row = (
        lax.broadcasted_iota(jnp.int32, (ROWS, points), 0) == spot // LANES
    ).astype(F32).astype(BF)
    at_col = lax.broadcasted_iota(jnp.int32, (LANES, points), 0) == lax.rem(spot, LANES)
    spread = jnp.where(at_col, value[...], 0.0)
    total = jnp.zeros((ROWS, LANES), F32)
    for piece in three_parts(spread):
        total = total + lax.dot_general(
            at_row, piece, (((1,), (1,)), ((), ())), preferred_element_type=F32
        )
    swath[...] = total * jnp.where(ch == 0, 1.0, 0.0)

    first_channel = lax.broadcasted_iota(jnp.int32, (WIDE, LANES), 0) == 0

    def cotan_rows(r):
        row = grad[r].astype(F32)
        row = row + jnp.where(first_channel, swath[pl.ds(r, 1), :], 0.0)
        cotan[r] = (row * mask[pl.ds(r, 1), :]).astype(BF)

    rows_loop(0, ROWS, cotan_rows)
    for q in range(4):
        scatter(q, cotan.at[pl.ds(SHARE * q, SHARE)], cot_all.at[ch], cs.at[q], cr.at[ch])
    for t in range(9):
        kb[t] = jnp.broadcast_to(taps[:, t : t + 1], (WIDE, LANES))

    wait_edges(0)
    send_rows(0, fwin)
    inner_windows(0, fwin)
    to_across.wait()
    passed.start()

    def conv_rows(low, high):
        for g in range(WIDE // 16):
            span = slice(16 * g, 16 * g + 16)
            ks = [kb[t, span, :] for t in range(9)]

            def body(r):
                acc = ks[0] * fwin[0, r, span, :]
                for t in range(1, 9):
                    acc = acc + ks[t] * fwin[t % 3, r + 2 * (t // 3), span, :]
                if g == WIDE // 16 - 1:
                    unit = lax.broadcasted_iota(jnp.int32, (16, LANES), 0) + 16 * g
                    acc = jnp.where(unit >= 75, 1.0, acc)
                conv[r, span, :] = acc.astype(BF)

            rows_loop(low, high, body)

    def send_conv(q):
        scatter(q, conv.at[pl.ds(SHARE * q, SHARE)], conv_all.at[ch], vs.at[q], vr.at[ch])

    conv_rows(SHARE, 3 * SHARE)
    send_conv(1)
    send_conv(2)
    wait_rows(0, fwin)
    conv_rows(0, SHARE)
    send_conv(0)
    conv_rows(3 * SHARE, 4 * SHARE)
    send_conv(3)

    to_mate.wait()
    acc_p[...] = jnp.zeros_like(acc_p)
    acc_e[...] = jnp.zeros_like(acc_e)
    rcopy(w_all.at[mate_across], w_all.at[mate_across], ws.at[2], wr.at[2], ch=mate).wait()
    for q in range(4):
        settle(q, cotan.at[pl.ds(SHARE * q, SHARE)], cot_all.at[q], cs.at[q], cr.at[q])
    for q in range(4):
        settle(q, conv.at[pl.ds(SHARE * q, SHARE)], conv_all.at[q], vs.at[q], vr.at[q])

    c0 = math.sqrt(2.0 / math.pi)

    def back_part(c, q):
        return cg_out.at[q, pl.ds(2 * c, 2)]

    def cells(c, unused):
        def both(ref):
            return jnp.concatenate(
                [
                    jnp.concatenate([ref[s, 2 * c + t] for s in range(4)], axis=0)
                    for t in range(2)
                ],
                axis=1,
            )

        x, y = both(conv_all), both(cot_all)
        w1 = w_all[:, 0].reshape(4 * UNITS, 4 * WIDE)
        w2 = w_all[:, 1].reshape(4 * UNITS, 4 * WIDE)
        h = jnp.dot(w1, x, preferred_element_type=F32)
        a = jnp.dot(w2, y, preferred_element_type=F32)
        square = h * h
        t = jnp.tanh(h * (c0 + (c0 * 0.044715) * square))
        half = 0.5 * t + 0.5
        activ = (h * half).astype(BF)
        slope = half + (0.5 * h) * (1.0 - t * t) * (c0 + (3.0 * c0 * 0.044715) * square)
        pre = (a * slope).astype(BF)
        acc_p[:, : 4 * WIDE] += lax.dot_general(activ, y, (((1,), (1,)), ((), ())), preferred_element_type=F32)
        acc_e[:, : 4 * WIDE] += lax.dot_general(pre, x, (((1,), (1,)), ((), ())), preferred_element_type=F32)
        back = lax.dot_general(w1, pre, (((0,), (0,)), ((), ())), preferred_element_type=F32).astype(BF)
        for q in range(4):
            for t in range(2):
                cg_out[q, 2 * c + t] = back[WIDE * q : WIDE * q + WIDE, LANES * t : LANES * t + LANES]
        for q in range(4):
            scatter(
                q, back_part(c, q), cg_in.at[pl.ds(SHARE * ch + 2 * c, 2)], gs.at[c, q], gr.at[c, ch]
            )
        return unused

    lax.fori_loop(0, SHARE // 2, cells, 0)

    for q in range(4):
        for which, ref in enumerate((acc_p, acc_e)):

            def body(d, unused):
                start = pl.multiple_of(UNITS * q + 8 * d, 8)
                for j in range(3):
                    place = pl.ds(pl.multiple_of(8 * (57 * which + 3 * d + j), 8), 8)
                    tiles[q, place, :] = ref[pl.ds(start, 8), LANES * j : LANES * j + LANES]
                return unused

            lax.fori_loop(0, 19, body, 0)

    used = pl.ds(0, 8 * TILES)
    pair = [
        rcopy(tiles.at[mate_across, used], pair_in.at[1], ps.at[1], pr.at[1], ch=mate),
        rcopy(tiles.at[mate, used], pair_in.at[0], ps.at[0], pr.at[0], ch=mate),
    ]
    for copy in pair:
        copy.start()

    for q in range(4):

        def body(c, unused):
            settle(q, back_part(c, q), cg_in.at[pl.ds(SHARE * q + 2 * c, 2)], gs.at[c, q], gr.at[c, q])
            return unused

        lax.fori_loop(0, SHARE // 2, body, 0)

    def grad_rows(r):
        gwin[1, 2 + r] = cg_in[r].astype(F32)

    rows_loop(0, ROWS, grad_rows)
    pack_edges(1, gwin)
    send_edges(1)

    def add_tiles(slot, ref, out=None):
        def body(d, unused):
            place = pl.ds(pl.multiple_of(48 * d, 16), 48)
            added = tiles[slot, place, :] + ref[place, :].astype(F32)
            if out is None:
                tiles[slot, place, :] = added
            else:
                out[place, :] = added.astype(BF)
            return unused

        lax.fori_loop(0, 8 * TILES // 48, body, 0)

    pair[0].wait()
    add_tiles(across, pair_in.at[1], cross_out)
    cross = rcopy(cross_out, cross_in, xs, xr, ch=across)
    cross.start()
    pair[1].wait()
    add_tiles(ch, pair_in.at[0])

    for g in range(REST):
        span = slice(8 * g, 8 * g + 8)

        def body(n, sums):
            for u in range(4):
                r = 4 * n + u
                now = gwin[1, 2 + r, span, :]
                sums = tuple(
                    sums[t] + now * fwin[t % 3, r + 2 * (t // 3), span, :] for t in range(9)
                )
            return sums

        sums = lax.fori_loop(0, ROWS // 4, body, tuple(jnp.zeros((8, LANES), F32) for _ in range(9)))
        spots = lax.broadcasted_iota(jnp.int32, (8, LANES), 1)
        kept = jnp.zeros((8, LANES), F32)
        for t in range(9):
            kept = jnp.where(spots == t, jnp.sum(sums[t], axis=1, keepdims=True), kept)
        tiles[ch, 8 * (TILES + g) : 8 * (TILES + g) + 8, :] = kept
    spare = 8 * (n_lat * n_lon - TILES - REST)
    tiles[ch, 8 * (TILES + REST) :, :] = jnp.zeros((spare, LANES), F32)

    wait_edges(1)
    send_rows(1, gwin)
    cross.wait()
    add_tiles(ch, cross_in)
    share = 8 * n_lon

    def lat_share(place):
        return pl.ds(pl.multiple_of(share * place, 16), share)

    def lon_share(place):
        return pl.ds(pl.multiple_of(8 * place, 8), 8)

    narrow[...] = tiles[ch].astype(BF)

    def lat_copies():
        return [
            rcopy(narrow.at[lat_share(lat_peer(s))], lat_in.at[s], send_a.at[s], recv_a.at[s], lat=lat_peer(s))
            for s in range(1, n_lat)
        ]

    for copy in lat_copies():
        copy.start()

    inner_windows(1, gwin)
    for copy in lat_copies():
        copy.wait()
    total = tiles[ch, lat_share(lat), :]
    for s in range(1, n_lat):
        total = total + lat_in[s].astype(F32)
    part[...] = total

    def lon_copies():
        return [
            rcopy(part.at[lon_share(lon_peer(s))], lon_in.at[s], send_b.at[s], recv_b.at[s], lon=lon_peer(s))
            for s in range(1, n_lon)
        ]

    for copy in lon_copies():
        copy.start()

    wait_rows(1, gwin)

    def adjoint_rows(low, high, rim):
        for g in range(WIDE // 16):
            span = slice(16 * g, 16 * g + 16)
            ks = [kb[8 - t, span, :] for t in range(9)]
            if rim:
                for b in range(3):
                    ks[6 + b] = jnp.where(top, kb[6 + b, span, :], ks[6 + b])

            def body(r):
                acc = cotan[r, span, :].astype(F32)
                for t in range(9):
                    acc = acc + ks[t] * gwin[t % 3, r + 2 * (t // 3), span, :]
                state_out[r, span, :] = (acc * mask[pl.ds(r, 1), :]).astype(BF)

            rows_loop(low, high, body, 2)

    adjoint_rows(0, ROWS // 2, False)
    for copy in lon_copies():
        copy.wait()
    total = part[lon_share(lon), :]
    for s in range(1, n_lon):
        total = total + lon_in[s]
    band[lon_share(lon), :] = total * scale

    def share_lon(s, source):
        piece = band.at[lon_share(source)]
        return rcopy(piece, piece, send_c.at[s], recv_c.at[s], lon=lon_peer(s))

    for s in range(1, n_lon):
        share_lon(s, lon).start()
    adjoint_rows(ROWS // 2, ROWS - 2, False)
    adjoint_rows(ROWS - 2, ROWS, True)
    for s in range(1, n_lon):
        share_lon(s, lon_peer(n_lon - s)).wait()
    whole[lat_share(lat), :] = band[...].astype(BF)

    def share_lat(s, source):
        piece = whole.at[lat_share(source)]
        return rcopy(piece, piece, send_d.at[s], recv_d.at[s], lat=lat_peer(s))

    for s in range(1, n_lat):
        share_lat(s, lat).start()
    for s in range(1, n_lat):
        share_lat(s, lat_peer(n_lat - s)).wait()
    final[...] = whole[...].astype(F32)

    def unpack(d, unused):
        start = pl.multiple_of(8 * d, 8)
        for which in range(2):
            for j in range(3):
                place = pl.ds(pl.multiple_of(8 * (57 * which + 3 * d + j), 8), 8)
                pad[which, pl.ds(start, 8), LANES * j : LANES * j + LANES] = final[place, :]
        return unused

    lax.fori_loop(0, 19, unpack, 0)
    for q in range(4):
        project_out[:, 75 * q : 75 * q + 75] = pad[0, :150, WIDE * q : WIDE * q + 75]
        expand_out[:, 75 * q : 75 * q + 75] = pad[1, :150, WIDE * q : WIDE * q + 75]
    bias_out[...] = pad[1, :, :LANES]
    kernel_out[...] = final[8 * TILES : 8 * (TILES + REST), :]


def on_device(
    ocean_state, land_mask, out_grad, swath_offset, swath_value,
    depth_kernel, expand_weight, expand_bias, project_weight,
):
    n_lon, n_lat = lax.axis_size("lon"), lax.axis_size("lat")
    channels = ocean_state.shape[0]
    units = expand_bias.shape[0]
    scale = 1.0 / math.sqrt(ROWS * n_lat * LANES * n_lon)
    extra = WIDE - channels

    def by_rows(x):
        return jnp.pad(jnp.transpose(x, (1, 0, 2)), ((0, 0), (0, extra), (0, 0)))

    taps = jnp.pad(depth_kernel.reshape(9, channels).T, ((0, extra), (0, LANES - 9)))

    def spread(w):
        w = w.reshape(units, 4, channels)
        return jnp.pad(w, ((0, UNITS - units), (0, 0), (0, extra)))

    high = lax.reduce_precision(expand_bias, 8, 7)
    middle = lax.reduce_precision(expand_bias - high, 8, 7)
    low = expand_bias - high - middle
    bias = jnp.stack([high, middle, low], axis=1).astype(BF)
    first = spread(expand_weight.T)
    bias = jnp.pad(bias[:, None, :], ((0, UNITS - units), (0, 3), (channels, extra - 3)))
    first = first + bias
    weights = jnp.stack([first, spread(project_weight)]).reshape(2, UNITS, 4 * WIDE)

    vmem = pl.BlockSpec(memory_space=pltpu.VMEM)
    block = (ROWS, WIDE, LANES)
    all_block = (4, SHARE, WIDE, LANES)
    all_rows = 8 * n_lat * n_lon
    dma = pltpu.SemaphoreType.DMA
    state, project, expand, bias_grad, kernel_grad = pl.pallas_call(
        functools.partial(step_kernel, scale, n_lon, n_lat),
        out_shape=[
            jax.ShapeDtypeStruct(block, BF),
            jax.ShapeDtypeStruct((units, 4 * channels), F32),
            jax.ShapeDtypeStruct((units, 4 * channels), F32),
            jax.ShapeDtypeStruct((152, LANES), F32),
            jax.ShapeDtypeStruct((WIDE, LANES), F32),
        ],
        in_specs=[vmem] * 7,
        out_specs=[vmem] * 5,
        scratch_shapes=[
            pltpu.VMEM((3, ROWS + 4, WIDE, LANES), F32),
            pltpu.VMEM((3, ROWS + 4, WIDE, LANES), F32),
            pltpu.VMEM((9, WIDE, LANES), F32),
            pltpu.VMEM((ROWS, LANES), F32),
            pltpu.VMEM(block, BF),
            pltpu.VMEM(block, BF),
            pltpu.VMEM(all_block, BF),
            pltpu.VMEM(all_block, BF),
            pltpu.VMEM((4, 2, UNITS, 4 * WIDE), BF),
            pltpu.VMEM((2, WIDE, LANES), BF),
            pltpu.VMEM((2, 2, WIDE, LANES), BF),
            pltpu.VMEM((2, WIDE, LANES), F32),
            pltpu.VMEM((2, 2, 3, WIDE, LANES), BF),
            pltpu.VMEM((2, 2, 3, WIDE, LANES), BF),
            pltpu.VMEM((4 * UNITS, 3 * LANES), F32),
            pltpu.VMEM((4 * UNITS, 3 * LANES), F32),
            pltpu.VMEM(all_block, BF),
            pltpu.VMEM(block, BF),
            pltpu.VMEM((4, all_rows, LANES), F32),
            pltpu.VMEM((2, 8 * TILES, LANES), F32),
            pltpu.VMEM((8 * TILES, LANES), BF),
            pltpu.VMEM((8 * TILES, LANES), BF),
            pltpu.VMEM((all_rows, LANES), BF),
            pltpu.VMEM((n_lat, 8 * n_lon, LANES), BF),
            pltpu.VMEM((8 * n_lon, LANES), F32),
            pltpu.VMEM((n_lon, 8, LANES), F32),
            pltpu.VMEM((8 * n_lon, LANES), F32),
            pltpu.VMEM((all_rows, LANES), BF),
            pltpu.VMEM((all_rows, LANES), F32),
            pltpu.VMEM((2, 152, 3 * LANES), F32),
        ]
        + [dma((2, 2))] * 4
        + [dma((3,))] * 2
        + [dma((4,))] * 4
        + [dma((4, 4))] * 2
        + [dma((2,))] * 2
        + [dma(())] * 2
        + [dma((n_lat,))] * 2
        + [dma((n_lon,))] * 4
        + [dma((n_lat,))] * 2,
        compiler_params=pltpu.CompilerParams(
            collective_id=0, has_side_effects=True, vmem_limit_bytes=56 * 2**20
        ),
    )(
        by_rows(ocean_state),
        by_rows(out_grad),
        land_mask.astype(F32),
        swath_offset.reshape(1, -1),
        swath_value.reshape(1, -1),
        taps,
        weights,
    )
    return (
        jnp.transpose(state[:, :channels], (1, 0, 2)),
        expand.T,
        project,
        bias_grad[:units, channels],
        kernel_grad[:channels, :9].T.reshape(3, 3, channels),
    )


def solution(mesh):
    return jax.shard_map(
        on_device,
        mesh=mesh,
        in_specs=(
            P("ch", "lat", "lon"),
            P("lat", "lon"),
            P("ch", "lat", "lon"),
            P("lat", "lon", None),
            P("lat", "lon", None),
            P(None, None, "ch"),
            P(None, "ch"),
            P("ch"),
            P("ch", None),
        ),
        out_specs=(
            P("ch", "lat", "lon"),
            P(None, "ch"),
            P("ch", None),
            P("ch"),
            P(None, None, "ch"),
        ),
        check_vma=False,
    )
```

```python
import functools
import math

import jax
import jax.numpy as jnp
from jax import lax
from jax.experimental import pallas as pl
from jax.experimental.pallas import tpu as pltpu
from jax.sharding import PartitionSpec as P

MESH = pl.DeviceIdType.MESH
ROWS = 32
WIDE = 80
LANES = 128
SHARE = 8
UNITS = 160
TILES = 114
REST = 10
BF = jnp.bfloat16
F32 = jnp.float32


def rcopy(src, dst, send, recv, **where):
    return pltpu.make_async_remote_copy(
        src, dst, send, recv, device_id=where, device_id_type=MESH
    )


def rows_loop(low, high, body, width=4):
    def several(n, unused):
        for t in range(width):
            body(low + n * width + t)
        return unused

    lax.fori_loop(0, (high - low) // width, several, 0)


def three_parts(x):
    high = x.astype(BF)
    left = x - high.astype(F32)
    middle = left.astype(BF)
    low = (left - middle.astype(F32)).astype(BF)
    return high, middle, low


def step_kernel(
    scale, n_lon, n_lat,
    state, grad, land, offset, value, taps, weights,
    state_out, project_out, expand_out, bias_out, kernel_out,
    fwin, gwin, kb, mask, tap_rows, swath, cotan, conv, cot_all, conv_all, w_all,
    pack_out, pack_in, side, msg_out, msg_in,
    acc_p, acc_e, cg_out, cg_in, tiles, pair_out, pair_in, cross_out, cross_in,
    narrow, lat_in, part, lon_in, band, whole, final, pad,
    es, er, ms, mr, ws, wr, cs, cr, vs, vr, gs, gr, ps, pr, xs, xr,
    send_a, recv_a, send_b, recv_b, send_c, recv_c, send_d, recv_d,
):
    lon, lat, ch = lax.axis_index("lon"), lax.axis_index("lat"), lax.axis_index("ch")
    top = lat == n_lat - 1
    mate = ch + 1 - 2 * lax.rem(ch, 2)
    across = lax.rem(ch + 2, 4)
    mate_across = lax.rem(mate + 2, 4)
    lane = lax.broadcasted_iota(jnp.int32, (WIDE, LANES), 1)

    def lat_peer(step):
        return lax.rem(lat + step, n_lat)

    def lon_peer(step):
        return lax.rem(lon + step, n_lon)

    barrier = pltpu.get_barrier_semaphore()
    for step in range(1, n_lat):
        pl.semaphore_signal(barrier, inc=1, device_id={"lat": lat_peer(step)}, device_id_type=MESH)
    for step in range(1, n_lon):
        pl.semaphore_signal(barrier, inc=1, device_id={"lon": lon_peer(step)}, device_id_type=MESH)
    for step in range(1, 4):
        pl.semaphore_signal(
            barrier, inc=1, device_id={"ch": lax.rem(ch + step, 4)}, device_id_type=MESH
        )

    def pack_edges(use, win):
        def body(r, acc):
            for t in range(4):
                row = 4 * r + t
                moved = pltpu.roll(win[1, 2 + row], lax.rem(4 * row + 2, LANES), 1)
                acc = jnp.where(lane // 4 == row, moved, acc)
            return acc

        pack_out[use] = lax.fori_loop(0, ROWS // 4, body, jnp.zeros((WIDE, LANES), F32)).astype(BF)

    def edge_copies(use):
        return [
            rcopy(pack_out.at[use], pack_in.at[use, 0], es.at[use, 0], er.at[use, 0], lon=lon_peer(1)),
            rcopy(pack_out.at[use], pack_in.at[use, 1], es.at[use, 1], er.at[use, 1], lon=lon_peer(n_lon - 1)),
        ]

    def send_edges(use):
        for copy in edge_copies(use):
            copy.start()

    def wait_edges(use):
        for copy in edge_copies(use):
            copy.wait()
        side[use] = jnp.where(
            lax.rem(lane, 4) < 2, pack_in[use, 0].astype(F32), pack_in[use, 1].astype(F32)
        )

    north_lat = jnp.minimum(lat + 1, n_lat - 1)
    north_lon = jnp.where(top, n_lon - 1 - lon, lon)
    north_slot = jnp.where(top, 1, 0)
    south_lat = jnp.maximum(lat - 1, 0)

    def north_copy(use):
        return rcopy(
            msg_out.at[use, 1], msg_in.at[use, north_slot], ms.at[use, 1], mr.at[use, north_slot],
            lat=north_lat, lon=north_lon,
        )

    def south_copy(use):
        return rcopy(
            msg_out.at[use, 0], msg_in.at[use, 1], ms.at[use, 0], mr.at[use, 1], lat=south_lat
        )

    def send_rows(use, win):
        edge = side[use]
        msg_out[use, 0, 0] = win[1, 2].astype(BF)
        msg_out[use, 0, 1] = win[1, 3].astype(BF)
        msg_out[use, 0, 2] = edge.astype(BF)

        @pl.when(lat > 0)
        def _():
            south_copy(use).start()

        @pl.when(jnp.logical_not(top))
        def _():
            msg_out[use, 1, 0] = win[1, ROWS].astype(BF)
            msg_out[use, 1, 1] = win[1, ROWS + 1].astype(BF)
            msg_out[use, 1, 2] = edge.astype(BF)

        @pl.when(top)
        def _():
            square = (LANES, LANES)
            turn = (
                lax.broadcasted_iota(jnp.int32, square, 0) + lax.broadcasted_iota(jnp.int32, square, 1)
                == LANES - 1
            ).astype(F32).astype(BF)
            for place, row in enumerate((win[1, ROWS + 1], win[1, ROWS], edge)):
                msg_out[use, 1, place] = jnp.dot(
                    row.astype(BF), turn, preferred_element_type=F32
                ).astype(BF)

        north_copy(use).start()

    def windows(win, p, quad, edge):
        x = win[1, p]
        win[0, p] = jnp.where(lane < 2, pltpu.roll(edge, lax.rem(LANES - 4 * quad, LANES), 1), pltpu.roll(x, 2, 1))
        win[2, p] = jnp.where(
            lane >= LANES - 2,
            pltpu.roll(edge, lax.rem(2 * LANES - 4 - 4 * quad, LANES), 1),
            pltpu.roll(x, LANES - 2, 1),
        )

    def inner_windows(use, win):
        edge = side[use]

        rows_loop(0, ROWS, lambda r: windows(win, r + 2, r, edge))

    def wait_rows(use, win):
        @pl.when(lat > 0)
        def _():
            south_copy(use).wait_send()
            rcopy(
                msg_out.at[use, 1], msg_in.at[use, 0], ms.at[use, 1], mr.at[use, 0], lat=south_lat
            ).wait_recv()

        @pl.when(lat == 0)
        def _():
            msg_in[use, 0] = jnp.zeros((3, WIDE, LANES), BF)

        north_copy(use).wait_send()
        rcopy(
            msg_out.at[use, 0], msg_in.at[use, 1], ms.at[use, 0], mr.at[use, 1],
            lat=north_lat, lon=north_lon,
        ).wait_recv()
        for slot, first, quad in ((0, 0, ROWS - 2), (1, ROWS + 2, 0)):
            edge = msg_in[use, slot, 2].astype(F32)
            for t in range(2):
                win[1, first + t] = msg_in[use, slot, t].astype(F32)
                windows(win, first + t, quad + t, edge)

    def scatter(q, src, dst, send, recv):
        @pl.when(ch != q)
        def _():
            rcopy(src, dst, send, recv, ch=jnp.int32(q)).start()

        @pl.when(ch == q)
        def _():
            dst[...] = src[...]

    def settle(q, src, dst, send, recv):
        @pl.when(ch != q)
        def _():
            rcopy(src, dst, send, recv, ch=jnp.int32(q)).wait()

    to_mate = rcopy(weights, w_all.at[ch], ws.at[0], wr.at[0], ch=mate)
    to_across = rcopy(weights, w_all.at[ch], ws.at[1], wr.at[1], ch=across)
    passed = rcopy(w_all.at[across], w_all.at[across], ws.at[2], wr.at[2], ch=mate)
    mask[...] = land[...].astype(F32)
    pl.semaphore_wait(barrier, n_lat + n_lon + 1)
    to_across.start()
    to_mate.start()

    def masked_rows(r):
        fwin[1, 2 + r] = state[r].astype(F32) * mask[pl.ds(r, 1), :]

    rows_loop(0, ROWS, masked_rows)
    pack_edges(0, fwin)
    send_edges(0)
    w_all[ch] = weights[...]

    spot = offset[...]
    points = spot.shape[1]
    at_row = (
        lax.broadcasted_iota(jnp.int32, (ROWS, points), 0) == spot // LANES
    ).astype(F32).astype(BF)
    at_col = lax.broadcasted_iota(jnp.int32, (LANES, points), 0) == lax.rem(spot, LANES)
    spread = jnp.where(at_col, value[...], 0.0)
    total = jnp.zeros((ROWS, LANES), F32)
    for piece in three_parts(spread):
        total = total + lax.dot_general(
            at_row, piece, (((1,), (1,)), ((), ())), preferred_element_type=F32
        )
    swath[...] = total * jnp.where(ch == 0, 1.0, 0.0)

    first_channel = lax.broadcasted_iota(jnp.int32, (WIDE, LANES), 0) == 0

    def cotan_rows(r):
        row = grad[r].astype(F32)
        row = row + jnp.where(first_channel, swath[pl.ds(r, 1), :], 0.0)
        cotan[r] = (row * mask[pl.ds(r, 1), :]).astype(BF)

    rows_loop(0, ROWS, cotan_rows)
    for q in range(4):
        scatter(q, cotan.at[pl.ds(SHARE * q, SHARE)], cot_all.at[ch], cs.at[q], cr.at[ch])
    tap_rows[...] = jnp.zeros_like(tap_rows)
    diagonal = lax.broadcasted_iota(jnp.int32, (WIDE, LANES), 0) == lane
    for t in range(9):
        tap_rows[t : t + 1, : taps.shape[2]] = taps[t // 3, t % 3 : t % 3 + 1, :]
    for t in range(9):
        column = jnp.where(diagonal, tap_rows[t : t + 1, :], 0.0)
        kb[t] = jnp.broadcast_to(jnp.sum(column, axis=1, keepdims=True), (WIDE, LANES))

    wait_edges(0)
    send_rows(0, fwin)
    inner_windows(0, fwin)
    to_across.wait()
    passed.start()

    def conv_piece(c):
        for g in range(WIDE // 16):
            span = slice(16 * g, 16 * g + 16)
            ks = [kb[t, span, :] for t in range(9)]
            for q in range(4):
                for r in (SHARE * q + 2 * c, SHARE * q + 2 * c + 1):
                    acc = ks[0] * fwin[0, r, span, :]
                    for t in range(1, 9):
                        acc = acc + ks[t] * fwin[t % 3, r + 2 * (t // 3), span, :]
                    if g == WIDE // 16 - 1:
                        unit = lax.broadcasted_iota(jnp.int32, (16, LANES), 0) + 16 * g
                        acc = jnp.where(unit >= 75, 1.0, acc)
                    conv[r, span, :] = acc.astype(BF)

    def conv_part(c, q):
        return conv.at[pl.ds(SHARE * q + 2 * c, 2)]

    def send_conv(c):
        for q in range(4):
            scatter(q, conv_part(c, q), conv_all.at[ch, pl.ds(2 * c, 2)], vs.at[c, q], vr.at[c, ch])

    for c in (1, 2):
        conv_piece(c)
        send_conv(c)
    wait_rows(0, fwin)
    for c in (3, 0):
        conv_piece(c)
        send_conv(c)

    to_mate.wait()
    acc_p[...] = jnp.zeros_like(acc_p)
    acc_e[...] = jnp.zeros_like(acc_e)
    rcopy(w_all.at[mate_across], w_all.at[mate_across], ws.at[2], wr.at[2], ch=mate).wait()
    for q in range(4):
        settle(q, cotan.at[pl.ds(SHARE * q, SHARE)], cot_all.at[q], cs.at[q], cr.at[q])

    c0 = math.sqrt(2.0 / math.pi)

    def back_part(c, q):
        return cg_out.at[q, pl.ds(2 * c, 2)]

    def cells(n, unused):
        c = lax.rem(n + 1, 4)
        for q in range(4):
            settle(q, conv_part(c, q), conv_all.at[q, pl.ds(2 * c, 2)], vs.at[c, q], vr.at[c, q])

        def both(ref):
            return jnp.concatenate(
                [
                    jnp.concatenate([ref[s, 2 * c + t] for s in range(4)], axis=0)
                    for t in range(2)
                ],
                axis=1,
            )

        x, y = both(conv_all), both(cot_all)
        w1 = w_all[:, 0].reshape(4 * UNITS, 4 * WIDE)
        w2 = w_all[:, 1].reshape(4 * UNITS, 4 * WIDE)
        h = jnp.dot(w1, x, preferred_element_type=F32)
        a = jnp.dot(w2, y, preferred_element_type=F32)
        square = h * h
        t = jnp.tanh(h * (c0 + (c0 * 0.044715) * square))
        half = 0.5 * t + 0.5
        activ = (h * half).astype(BF)
        slope = half + (0.5 * h) * (1.0 - t * t) * (c0 + (3.0 * c0 * 0.044715) * square)
        pre = (a * slope).astype(BF)
        acc_p[:, : 4 * WIDE] += lax.dot_general(activ, y, (((1,), (1,)), ((), ())), preferred_element_type=F32)
        acc_e[:, : 4 * WIDE] += lax.dot_general(pre, x, (((1,), (1,)), ((), ())), preferred_element_type=F32)
        back = lax.dot_general(w1, pre, (((0,), (0,)), ((), ())), preferred_element_type=F32).astype(BF)
        for q in range(4):
            for t in range(2):
                cg_out[q, 2 * c + t] = back[WIDE * q : WIDE * q + WIDE, LANES * t : LANES * t + LANES]
        for q in range(4):
            scatter(
                q, back_part(c, q), cg_in.at[pl.ds(SHARE * ch + 2 * c, 2)], gs.at[c, q], gr.at[c, ch]
            )
        return unused

    lax.fori_loop(0, SHARE // 2, cells, 0)

    for q in range(4):
        for which, ref in enumerate((acc_p, acc_e)):

            def body(d, unused):
                start = pl.multiple_of(UNITS * q + 8 * d, 8)
                for j in range(3):
                    place = pl.ds(pl.multiple_of(8 * (57 * which + 3 * d + j), 8), 8)
                    tiles[q, place, :] = ref[pl.ds(start, 8), LANES * j : LANES * j + LANES]
                return unused

            lax.fori_loop(0, 19, body, 0)

    used = pl.ds(0, 8 * TILES)
    pair_out[1] = tiles[mate_across, used, :].astype(BF)
    pair_out[0] = tiles[mate, used, :].astype(BF)
    pair = [
        rcopy(pair_out.at[1], pair_in.at[1], ps.at[1], pr.at[1], ch=mate),
        rcopy(pair_out.at[0], pair_in.at[0], ps.at[0], pr.at[0], ch=mate),
    ]
    for copy in pair:
        copy.start()

    for q in range(4):

        def body(c, unused):
            settle(q, back_part(c, q), cg_in.at[pl.ds(SHARE * q + 2 * c, 2)], gs.at[c, q], gr.at[c, q])
            return unused

        lax.fori_loop(0, SHARE // 2, body, 0)

    def grad_rows(r):
        gwin[1, 2 + r] = cg_in[r].astype(F32)

    rows_loop(0, ROWS, grad_rows)
    pack_edges(1, gwin)
    send_edges(1)

    def add_tiles(slot, ref, out=None):
        def body(d, unused):
            place = pl.ds(pl.multiple_of(48 * d, 16), 48)
            added = tiles[slot, place, :] + ref[place, :].astype(F32)
            if out is None:
                tiles[slot, place, :] = added
            else:
                out[place, :] = added.astype(BF)
            return unused

        lax.fori_loop(0, 8 * TILES // 48, body, 0)

    pair[0].wait()
    add_tiles(across, pair_in.at[1], cross_out)
    cross = rcopy(cross_out, cross_in, xs, xr, ch=across)
    cross.start()
    pair[1].wait()
    add_tiles(ch, pair_in.at[0])

    for g in range(REST):
        span = slice(8 * g, 8 * g + 8)

        def body(n, sums):
            for u in range(4):
                r = 4 * n + u
                now = gwin[1, 2 + r, span, :]
                sums = tuple(
                    sums[t] + now * fwin[t % 3, r + 2 * (t // 3), span, :] for t in range(9)
                )
            return sums

        sums = lax.fori_loop(0, ROWS // 4, body, tuple(jnp.zeros((8, LANES), F32) for _ in range(9)))
        spots = lax.broadcasted_iota(jnp.int32, (8, LANES), 1)
        kept = jnp.zeros((8, LANES), F32)
        for t in range(9):
            kept = jnp.where(spots == t, jnp.sum(sums[t], axis=1, keepdims=True), kept)
        tiles[ch, 8 * (TILES + g) : 8 * (TILES + g) + 8, :] = kept
    spare = 8 * (n_lat * n_lon - TILES - REST)
    tiles[ch, 8 * (TILES + REST) :, :] = jnp.zeros((spare, LANES), F32)

    wait_edges(1)
    send_rows(1, gwin)
    cross.wait()
    add_tiles(ch, cross_in)
    share = 8 * n_lon

    def lat_share(place):
        return pl.ds(pl.multiple_of(share * place, 16), share)

    def lon_share(place):
        return pl.ds(pl.multiple_of(8 * place, 8), 8)

    narrow[...] = tiles[ch].astype(BF)

    def lat_copies():
        return [
            rcopy(narrow.at[lat_share(lat_peer(s))], lat_in.at[s], send_a.at[s], recv_a.at[s], lat=lat_peer(s))
            for s in range(1, n_lat)
        ]

    for copy in lat_copies():
        copy.start()

    inner_windows(1, gwin)
    for copy in lat_copies():
        copy.wait()
    total = tiles[ch, lat_share(lat), :]
    for s in range(1, n_lat):
        total = total + lat_in[s].astype(F32)
    part[...] = total

    def lon_copies():
        return [
            rcopy(part.at[lon_share(lon_peer(s))], lon_in.at[s], send_b.at[s], recv_b.at[s], lon=lon_peer(s))
            for s in range(1, n_lon)
        ]

    for copy in lon_copies():
        copy.start()

    wait_rows(1, gwin)

    def adjoint_rows(low, high, rim):
        for g in range(WIDE // 16):
            span = slice(16 * g, 16 * g + 16)
            ks = [kb[8 - t, span, :] for t in range(9)]
            if rim:
                for b in range(3):
                    ks[6 + b] = jnp.where(top, kb[6 + b, span, :], ks[6 + b])

            def body(r):
                acc = cotan[r, span, :].astype(F32)
                for t in range(9):
                    acc = acc + ks[t] * gwin[t % 3, r + 2 * (t // 3), span, :]
                state_out[r, span, :] = (acc * mask[pl.ds(r, 1), :]).astype(BF)

            rows_loop(low, high, body, 2)

    adjoint_rows(0, ROWS // 2, False)
    for copy in lon_copies():
        copy.wait()
    total = part[lon_share(lon), :]
    for s in range(1, n_lon):
        total = total + lon_in[s]
    band[lon_share(lon), :] = total * scale

    def share_lon(s, source):
        piece = band.at[lon_share(source)]
        return rcopy(piece, piece, send_c.at[s], recv_c.at[s], lon=lon_peer(s))

    for s in range(1, n_lon):
        share_lon(s, lon).start()
    adjoint_rows(ROWS // 2, ROWS - 2, False)
    adjoint_rows(ROWS - 2, ROWS, True)
    for s in range(1, n_lon):
        share_lon(s, lon_peer(n_lon - s)).wait()
    whole[lat_share(lat), :] = band[...].astype(BF)

    def share_lat(s, source):
        piece = whole.at[lat_share(source)]
        return rcopy(piece, piece, send_d.at[s], recv_d.at[s], lat=lat_peer(s))

    for s in range(1, n_lat):
        share_lat(s, lat).start()
    for s in range(1, n_lat):
        share_lat(s, lat_peer(n_lat - s)).wait()
    final[...] = whole[...].astype(F32)

    def unpack(d, unused):
        start = pl.multiple_of(8 * d, 8)
        for which in range(2):
            for j in range(3):
                place = pl.ds(pl.multiple_of(8 * (57 * which + 3 * d + j), 8), 8)
                pad[which, pl.ds(start, 8), LANES * j : LANES * j + LANES] = final[place, :]
        return unused

    lax.fori_loop(0, 19, unpack, 0)
    for q in range(4):
        project_out[:, 75 * q : 75 * q + 75] = pad[0, :150, WIDE * q : WIDE * q + 75]
        expand_out[:, 75 * q : 75 * q + 75] = pad[1, :150, WIDE * q : WIDE * q + 75]
    bias_out[...] = pad[1, :, :LANES]
    kernel_out[...] = final[8 * TILES : 8 * (TILES + REST), :]


def on_device(
    ocean_state, land_mask, out_grad, swath_offset, swath_value,
    depth_kernel, expand_weight, expand_bias, project_weight,
):
    n_lon, n_lat = lax.axis_size("lon"), lax.axis_size("lat")
    channels = ocean_state.shape[0]
    units = expand_bias.shape[0]
    scale = 1.0 / math.sqrt(ROWS * n_lat * LANES * n_lon)
    extra = WIDE - channels

    def by_rows(x):
        return jnp.pad(jnp.transpose(x, (1, 0, 2)), ((0, 0), (0, extra), (0, 0)))


    def spread(w):
        w = w.reshape(units, 4, channels)
        return jnp.pad(w, ((0, UNITS - units), (0, 0), (0, extra)))

    high = lax.reduce_precision(expand_bias, 8, 7)
    middle = lax.reduce_precision(expand_bias - high, 8, 7)
    low = expand_bias - high - middle
    bias = jnp.stack([high, middle, low], axis=1).astype(BF)
    first = spread(expand_weight.T)
    bias = jnp.pad(bias[:, None, :], ((0, UNITS - units), (0, 3), (channels, extra - 3)))
    first = first + bias
    weights = jnp.stack([first, spread(project_weight)]).reshape(2, UNITS, 4 * WIDE)

    vmem = pl.BlockSpec(memory_space=pltpu.VMEM)
    block = (ROWS, WIDE, LANES)
    all_block = (4, SHARE, WIDE, LANES)
    all_rows = 8 * n_lat * n_lon
    dma = pltpu.SemaphoreType.DMA
    state, project, expand, bias_grad, kernel_grad = pl.pallas_call(
        functools.partial(step_kernel, scale, n_lon, n_lat),
        out_shape=[
            jax.ShapeDtypeStruct(block, BF),
            jax.ShapeDtypeStruct((units, 4 * channels), F32),
            jax.ShapeDtypeStruct((units, 4 * channels), F32),
            jax.ShapeDtypeStruct((152, LANES), F32),
            jax.ShapeDtypeStruct((WIDE, LANES), F32),
        ],
        in_specs=[vmem] * 7,
        out_specs=[vmem] * 5,
        scratch_shapes=[
            pltpu.VMEM((3, ROWS + 4, WIDE, LANES), F32),
            pltpu.VMEM((3, ROWS + 4, WIDE, LANES), F32),
            pltpu.VMEM((9, WIDE, LANES), F32),
            pltpu.VMEM((ROWS, LANES), F32),
            pltpu.VMEM((16, LANES), F32),
            pltpu.VMEM((ROWS, LANES), F32),
            pltpu.VMEM(block, BF),
            pltpu.VMEM(block, BF),
            pltpu.VMEM(all_block, BF),
            pltpu.VMEM(all_block, BF),
            pltpu.VMEM((4, 2, UNITS, 4 * WIDE), BF),
            pltpu.VMEM((2, WIDE, LANES), BF),
            pltpu.VMEM((2, 2, WIDE, LANES), BF),
            pltpu.VMEM((2, WIDE, LANES), F32),
            pltpu.VMEM((2, 2, 3, WIDE, LANES), BF),
            pltpu.VMEM((2, 2, 3, WIDE, LANES), BF),
            pltpu.VMEM((4 * UNITS, 3 * LANES), F32),
            pltpu.VMEM((4 * UNITS, 3 * LANES), F32),
            pltpu.VMEM(all_block, BF),
            pltpu.VMEM(block, BF),
            pltpu.VMEM((4, all_rows, LANES), F32),
            pltpu.VMEM((2, 8 * TILES, LANES), BF),
            pltpu.VMEM((2, 8 * TILES, LANES), BF),
            pltpu.VMEM((8 * TILES, LANES), BF),
            pltpu.VMEM((8 * TILES, LANES), BF),
            pltpu.VMEM((all_rows, LANES), BF),
            pltpu.VMEM((n_lat, 8 * n_lon, LANES), BF),
            pltpu.VMEM((8 * n_lon, LANES), F32),
            pltpu.VMEM((n_lon, 8, LANES), F32),
            pltpu.VMEM((8 * n_lon, LANES), F32),
            pltpu.VMEM((all_rows, LANES), BF),
            pltpu.VMEM((all_rows, LANES), F32),
            pltpu.VMEM((2, 152, 3 * LANES), F32),
        ]
        + [dma((2, 2))] * 4
        + [dma((3,))] * 2
        + [dma((4,))] * 2
        + [dma((4, 4))] * 4
        + [dma((2,))] * 2
        + [dma(())] * 2
        + [dma((n_lat,))] * 2
        + [dma((n_lon,))] * 4
        + [dma((n_lat,))] * 2,
        compiler_params=pltpu.CompilerParams(
            collective_id=0, has_side_effects=True, vmem_limit_bytes=56 * 2**20
        ),
    )(
        by_rows(ocean_state),
        by_rows(out_grad),
        land_mask,
        swath_offset.reshape(1, -1),
        swath_value.reshape(1, -1),
        depth_kernel,
        weights,
    )
    return (
        jnp.transpose(state[:, :channels], (1, 0, 2)),
        expand.T,
        project,
        bias_grad[:units, channels],
        kernel_grad[:channels, :9].T.reshape(3, 3, channels),
    )


def solution(mesh):
    return jax.shard_map(
        on_device,
        mesh=mesh,
        in_specs=(
            P("ch", "lat", "lon"),
            P("lat", "lon"),
            P("ch", "lat", "lon"),
            P("lat", "lon", None),
            P("lat", "lon", None),
            P(None, None, "ch"),
            P(None, "ch"),
            P("ch"),
            P("ch", None),
        ),
        out_specs=(
            P("ch", "lat", "lon"),
            P(None, "ch"),
            P("ch", None),
            P("ch"),
            P(None, None, "ch"),
        ),
        check_vma=False,
    )
```

```python
import functools
import math

import jax
import jax.numpy as jnp
from jax import lax
from jax.experimental import pallas as pl
from jax.experimental.pallas import tpu as pltpu
from jax.sharding import PartitionSpec as P

MESH = pl.DeviceIdType.MESH
ROWS = 32
WIDE = 80
LANES = 128
SHARE = 8
UNITS = 160
TILES = 114
REST = 10
BF = jnp.bfloat16
F32 = jnp.float32


def rcopy(src, dst, send, recv, **where):
    return pltpu.make_async_remote_copy(
        src, dst, send, recv, device_id=where, device_id_type=MESH
    )


def rows_loop(low, high, body, width=4):
    def several(n, unused):
        for t in range(width):
            body(low + n * width + t)
        return unused

    lax.fori_loop(0, (high - low) // width, several, 0)


def three_parts(x):
    high = x.astype(BF)
    left = x - high.astype(F32)
    middle = left.astype(BF)
    low = (left - middle.astype(F32)).astype(BF)
    return high, middle, low


def step_kernel(
    scale, n_lon, n_lat,
    state, grad, land, offset, value, taps, weights,
    state_out, project_out, expand_out, bias_out, kernel_out,
    fwin, gwin, kb, mask, tap_rows, swath, cotan, conv, cot_all, conv_all, w_all,
    pack_out, pack_in, side, msg_out, msg_in,
    acc_p, acc_e, cg_out, cg_in, tiles, pair_out, pair_in, cross_out, cross_in,
    narrow, lat_in, part, lon_in, band, whole, final, pad,
    es, er, ms, mr, ws, wr, cs, cr, vs, vr, gs, gr, ps, pr, xs, xr,
    send_a, recv_a, send_b, recv_b, send_c, recv_c, send_d, recv_d,
):
    lon, lat, ch = lax.axis_index("lon"), lax.axis_index("lat"), lax.axis_index("ch")
    top = lat == n_lat - 1
    mate = ch + 1 - 2 * lax.rem(ch, 2)
    across = lax.rem(ch + 2, 4)
    mate_across = lax.rem(mate + 2, 4)
    far = lax.rem(lat + n_lat // 2, n_lat)
    lane = lax.broadcasted_iota(jnp.int32, (WIDE, LANES), 1)

    def lat_peer(step):
        return lax.rem(lat + step, n_lat)

    def lon_peer(step):
        return lax.rem(lon + step, n_lon)

    barrier = pltpu.get_barrier_semaphore()
    for step in range(1, n_lat):
        pl.semaphore_signal(barrier, inc=1, device_id={"lat": lat_peer(step)}, device_id_type=MESH)
    for step in range(1, n_lon):
        pl.semaphore_signal(barrier, inc=1, device_id={"lon": lon_peer(step)}, device_id_type=MESH)
    for step in range(1, 4):
        pl.semaphore_signal(
            barrier, inc=1, device_id={"ch": lax.rem(ch + step, 4)}, device_id_type=MESH
        )
    pl.semaphore_signal(
        barrier, inc=1, device_id={"ch": across, "lat": far}, device_id_type=MESH
    )

    def pack_edges(use, win):
        def body(r, acc):
            for t in range(4):
                row = 4 * r + t
                moved = pltpu.roll(win[1, 2 + row], lax.rem(4 * row + 2, LANES), 1)
                acc = jnp.where(lane // 4 == row, moved, acc)
            return acc

        pack_out[use] = lax.fori_loop(0, ROWS // 4, body, jnp.zeros((WIDE, LANES), F32)).astype(BF)

    def edge_copies(use):
        return [
            rcopy(pack_out.at[use], pack_in.at[use, 0], es.at[use, 0], er.at[use, 0], lon=lon_peer(1)),
            rcopy(pack_out.at[use], pack_in.at[use, 1], es.at[use, 1], er.at[use, 1], lon=lon_peer(n_lon - 1)),
        ]

    def send_edges(use):
        for copy in edge_copies(use):
            copy.start()

    def wait_edges(use):
        for copy in edge_copies(use):
            copy.wait()
        side[use] = jnp.where(
            lax.rem(lane, 4) < 2, pack_in[use, 0].astype(F32), pack_in[use, 1].astype(F32)
        )

    north_lat = jnp.minimum(lat + 1, n_lat - 1)
    north_lon = jnp.where(top, n_lon - 1 - lon, lon)
    north_slot = jnp.where(top, 1, 0)
    south_lat = jnp.maximum(lat - 1, 0)

    def north_copy(use):
        return rcopy(
            msg_out.at[use, 1], msg_in.at[use, north_slot], ms.at[use, 1], mr.at[use, north_slot],
            lat=north_lat, lon=north_lon,
        )

    def south_copy(use):
        return rcopy(
            msg_out.at[use, 0], msg_in.at[use, 1], ms.at[use, 0], mr.at[use, 1], lat=south_lat
        )

    def send_rows(use, win):
        edge = side[use]
        msg_out[use, 0, 0] = win[1, 2].astype(BF)
        msg_out[use, 0, 1] = win[1, 3].astype(BF)
        msg_out[use, 0, 2] = edge.astype(BF)

        @pl.when(lat > 0)
        def _():
            south_copy(use).start()

        @pl.when(jnp.logical_not(top))
        def _():
            msg_out[use, 1, 0] = win[1, ROWS].astype(BF)
            msg_out[use, 1, 1] = win[1, ROWS + 1].astype(BF)
            msg_out[use, 1, 2] = edge.astype(BF)

        @pl.when(top)
        def _():
            square = (LANES, LANES)
            turn = (
                lax.broadcasted_iota(jnp.int32, square, 0) + lax.broadcasted_iota(jnp.int32, square, 1)
                == LANES - 1
            ).astype(F32).astype(BF)
            for place, row in enumerate((win[1, ROWS + 1], win[1, ROWS], edge)):
                msg_out[use, 1, place] = jnp.dot(
                    row.astype(BF), turn, preferred_element_type=F32
                ).astype(BF)

        north_copy(use).start()

    def windows(win, p, quad, edge):
        x = win[1, p]
        win[0, p] = jnp.where(lane < 2, pltpu.roll(edge, lax.rem(LANES - 4 * quad, LANES), 1), pltpu.roll(x, 2, 1))
        win[2, p] = jnp.where(
            lane >= LANES - 2,
            pltpu.roll(edge, lax.rem(2 * LANES - 4 - 4 * quad, LANES), 1),
            pltpu.roll(x, LANES - 2, 1),
        )

    def inner_windows(use, win):
        edge = side[use]

        rows_loop(0, ROWS, lambda r: windows(win, r + 2, r, edge))

    def wait_rows(use, win):
        @pl.when(lat > 0)
        def _():
            south_copy(use).wait_send()
            rcopy(
                msg_out.at[use, 1], msg_in.at[use, 0], ms.at[use, 1], mr.at[use, 0], lat=south_lat
            ).wait_recv()

        @pl.when(lat == 0)
        def _():
            msg_in[use, 0] = jnp.zeros((3, WIDE, LANES), BF)

        north_copy(use).wait_send()
        rcopy(
            msg_out.at[use, 0], msg_in.at[use, 1], ms.at[use, 0], mr.at[use, 1],
            lat=north_lat, lon=north_lon,
        ).wait_recv()
        for slot, first, quad in ((0, 0, ROWS - 2), (1, ROWS + 2, 0)):
            edge = msg_in[use, slot, 2].astype(F32)
            for t in range(2):
                win[1, first + t] = msg_in[use, slot, t].astype(F32)
                windows(win, first + t, quad + t, edge)

    def scatter(q, src, dst, send, recv):
        @pl.when(ch != q)
        def _():
            rcopy(src, dst, send, recv, ch=jnp.int32(q)).start()

        @pl.when(ch == q)
        def _():
            dst[...] = src[...]

    def settle(q, src, dst, send, recv):
        @pl.when(ch != q)
        def _():
            rcopy(src, dst, send, recv, ch=jnp.int32(q)).wait()

    to_mate = rcopy(weights, w_all.at[ch], ws.at[0], wr.at[0], ch=mate)
    to_across = rcopy(weights, w_all.at[ch], ws.at[1], wr.at[1], ch=across, lat=far)
    passed = rcopy(w_all.at[across], w_all.at[across], ws.at[2], wr.at[2], ch=mate)
    mask[...] = land[...].astype(F32)
    pl.semaphore_wait(barrier, n_lat + n_lon + 2)
    to_across.start()
    to_mate.start()

    def masked_rows(r):
        fwin[1, 2 + r] = state[r].astype(F32) * mask[pl.ds(r, 1), :]

    rows_loop(0, ROWS, masked_rows)
    pack_edges(0, fwin)
    send_edges(0)
    w_all[ch] = weights[...]

    spot = offset[...]
    points = spot.shape[1]
    at_row = (
        lax.broadcasted_iota(jnp.int32, (ROWS, points), 0) == spot // LANES
    ).astype(F32).astype(BF)
    at_col = lax.broadcasted_iota(jnp.int32, (LANES, points), 0) == lax.rem(spot, LANES)
    spread = jnp.where(at_col, value[...], 0.0)
    total = jnp.zeros((ROWS, LANES), F32)
    for piece in three_parts(spread):
        total = total + lax.dot_general(
            at_row, piece, (((1,), (1,)), ((), ())), preferred_element_type=F32
        )
    swath[...] = total * jnp.where(ch == 0, 1.0, 0.0)

    first_channel = lax.broadcasted_iota(jnp.int32, (WIDE, LANES), 0) == 0

    def cotan_rows(r):
        row = grad[r].astype(F32)
        row = row + jnp.where(first_channel, swath[pl.ds(r, 1), :], 0.0)
        cotan[r] = (row * mask[pl.ds(r, 1), :]).astype(BF)

    rows_loop(0, ROWS, cotan_rows)
    for q in range(4):
        scatter(q, cotan.at[pl.ds(SHARE * q, SHARE)], cot_all.at[ch], cs.at[q], cr.at[ch])
    tap_rows[...] = jnp.zeros_like(tap_rows)
    diagonal = lax.broadcasted_iota(jnp.int32, (WIDE, LANES), 0) == lane
    for t in range(9):
        tap_rows[t : t + 1, : taps.shape[2]] = taps[t // 3, t % 3 : t % 3 + 1, :]
    for t in range(9):
        column = jnp.where(diagonal, tap_rows[t : t + 1, :], 0.0)
        kb[t] = jnp.broadcast_to(jnp.sum(column, axis=1, keepdims=True), (WIDE, LANES))

    wait_edges(0)
    send_rows(0, fwin)
    inner_windows(0, fwin)
    to_across.wait()
    passed.start()

    def conv_piece(c):
        for g in range(WIDE // 16):
            span = slice(16 * g, 16 * g + 16)
            ks = [kb[t, span, :] for t in range(9)]
            for q in range(4):
                for r in (SHARE * q + 2 * c, SHARE * q + 2 * c + 1):
                    acc = ks[0] * fwin[0, r, span, :]
                    for t in range(1, 9):
                        acc = acc + ks[t] * fwin[t % 3, r + 2 * (t // 3), span, :]
                    if g == WIDE // 16 - 1:
                        unit = lax.broadcasted_iota(jnp.int32, (16, LANES), 0) + 16 * g
                        acc = jnp.where(unit >= 75, 1.0, acc)
                    conv[r, span, :] = acc.astype(BF)

    def conv_part(c, q):
        return conv.at[pl.ds(SHARE * q + 2 * c, 2)]

    def send_conv(c):
        for q in range(4):
            scatter(q, conv_part(c, q), conv_all.at[ch, pl.ds(2 * c, 2)], vs.at[c, q], vr.at[c, ch])

    for c in (1, 2):
        conv_piece(c)
        send_conv(c)
    wait_rows(0, fwin)
    for c in (3, 0):
        conv_piece(c)
        send_conv(c)

    to_mate.wait()
    acc_p[...] = jnp.zeros_like(acc_p)
    acc_e[...] = jnp.zeros_like(acc_e)
    rcopy(w_all.at[mate_across], w_all.at[mate_across], ws.at[2], wr.at[2], ch=mate).wait()
    for q in range(4):
        settle(q, cotan.at[pl.ds(SHARE * q, SHARE)], cot_all.at[q], cs.at[q], cr.at[q])

    c0 = math.sqrt(2.0 / math.pi)

    def back_part(c, q):
        return cg_out.at[q, pl.ds(2 * c, 2)]

    def cells(n, unused):
        c = lax.rem(n + 1, 4)
        for q in range(4):
            settle(q, conv_part(c, q), conv_all.at[q, pl.ds(2 * c, 2)], vs.at[c, q], vr.at[c, q])

        def both(ref):
            return jnp.concatenate(
                [
                    jnp.concatenate([ref[s, 2 * c + t] for s in range(4)], axis=0)
                    for t in range(2)
                ],
                axis=1,
            )

        x, y = both(conv_all), both(cot_all)
        w1 = w_all[:, 0].reshape(4 * UNITS, 4 * WIDE)
        w2 = w_all[:, 1].reshape(4 * UNITS, 4 * WIDE)
        h = jnp.dot(w1, x, preferred_element_type=F32)
        a = jnp.dot(w2, y, preferred_element_type=F32)
        square = h * h
        t = jnp.tanh(h * (c0 + (c0 * 0.044715) * square))
        half = 0.5 * t + 0.5
        activ = (h * half).astype(BF)
        slope = half + (0.5 * h) * (1.0 - t * t) * (c0 + (3.0 * c0 * 0.044715) * square)
        pre = (a * slope).astype(BF)
        acc_p[:, : 4 * WIDE] += lax.dot_general(activ, y, (((1,), (1,)), ((), ())), preferred_element_type=F32)
        acc_e[:, : 4 * WIDE] += lax.dot_general(pre, x, (((1,), (1,)), ((), ())), preferred_element_type=F32)
        back = lax.dot_general(w1, pre, (((0,), (0,)), ((), ())), preferred_element_type=F32).astype(BF)
        for q in range(4):
            for t in range(2):
                cg_out[q, 2 * c + t] = back[WIDE * q : WIDE * q + WIDE, LANES * t : LANES * t + LANES]
        for q in range(4):
            scatter(
                q, back_part(c, q), cg_in.at[pl.ds(SHARE * ch + 2 * c, 2)], gs.at[c, q], gr.at[c, ch]
            )
        return unused

    lax.fori_loop(0, SHARE // 2, cells, 0)

    for q in range(4):
        for which, ref in enumerate((acc_p, acc_e)):

            def body(d, unused):
                start = pl.multiple_of(UNITS * q + 8 * d, 8)
                for j in range(3):
                    place = pl.ds(pl.multiple_of(8 * (57 * which + 3 * d + j), 8), 8)
                    tiles[q, place, :] = ref[pl.ds(start, 8), LANES * j : LANES * j + LANES]
                return unused

            lax.fori_loop(0, 19, body, 0)

    used = pl.ds(0, 8 * TILES)
    pair_out[1] = tiles[mate_across, used, :].astype(BF)
    pair_out[0] = tiles[mate, used, :].astype(BF)
    pair = [
        rcopy(pair_out.at[1], pair_in.at[1], ps.at[1], pr.at[1], ch=mate),
        rcopy(pair_out.at[0], pair_in.at[0], ps.at[0], pr.at[0], ch=mate),
    ]
    for copy in pair:
        copy.start()

    for q in range(4):

        def body(c, unused):
            settle(q, back_part(c, q), cg_in.at[pl.ds(SHARE * q + 2 * c, 2)], gs.at[c, q], gr.at[c, q])
            return unused

        lax.fori_loop(0, SHARE // 2, body, 0)

    def grad_rows(r):
        gwin[1, 2 + r] = cg_in[r].astype(F32)

    rows_loop(0, ROWS, grad_rows)
    pack_edges(1, gwin)
    send_edges(1)

    def add_tiles(slot, ref, out=None):
        def body(d, unused):
            place = pl.ds(pl.multiple_of(48 * d, 16), 48)
            added = tiles[slot, place, :] + ref[place, :].astype(F32)
            if out is None:
                tiles[slot, place, :] = added
            else:
                out[place, :] = added.astype(BF)
            return unused

        lax.fori_loop(0, 8 * TILES // 48, body, 0)

    pair[0].wait()
    add_tiles(across, pair_in.at[1], cross_out)
    cross = rcopy(cross_out, cross_in, xs, xr, ch=across, lat=far)
    cross.start()
    pair[1].wait()
    add_tiles(ch, pair_in.at[0])

    for g in range(REST):
        span = slice(8 * g, 8 * g + 8)

        def body(n, sums):
            for u in range(4):
                r = 4 * n + u
                now = gwin[1, 2 + r, span, :]
                sums = tuple(
                    sums[t] + now * fwin[t % 3, r + 2 * (t // 3), span, :] for t in range(9)
                )
            return sums

        sums = lax.fori_loop(0, ROWS // 4, body, tuple(jnp.zeros((8, LANES), F32) for _ in range(9)))
        spots = lax.broadcasted_iota(jnp.int32, (8, LANES), 1)
        kept = jnp.zeros((8, LANES), F32)
        for t in range(9):
            kept = jnp.where(spots == t, jnp.sum(sums[t], axis=1, keepdims=True), kept)
        tiles[ch, 8 * (TILES + g) : 8 * (TILES + g) + 8, :] = kept
    spare = 8 * (n_lat * n_lon - TILES - REST)
    tiles[ch, 8 * (TILES + REST) :, :] = jnp.zeros((spare, LANES), F32)

    wait_edges(1)
    send_rows(1, gwin)
    cross.wait()
    add_tiles(ch, cross_in)
    share = 8 * n_lon

    def lat_share(place):
        return pl.ds(pl.multiple_of(share * place, 16), share)

    def lon_share(place):
        return pl.ds(pl.multiple_of(8 * place, 8), 8)

    narrow[...] = tiles[ch].astype(BF)

    def lat_copies():
        return [
            rcopy(narrow.at[lat_share(lat_peer(s))], lat_in.at[s], send_a.at[s], recv_a.at[s], lat=lat_peer(s))
            for s in range(1, n_lat)
        ]

    for copy in lat_copies():
        copy.start()

    inner_windows(1, gwin)
    for copy in lat_copies():
        copy.wait()
    total = tiles[ch, lat_share(lat), :]
    for s in range(1, n_lat):
        total = total + lat_in[s].astype(F32)
    part[...] = total

    def lon_copies():
        return [
            rcopy(part.at[lon_share(lon_peer(s))], lon_in.at[s], send_b.at[s], recv_b.at[s], lon=lon_peer(s))
            for s in range(1, n_lon)
        ]

    for copy in lon_copies():
        copy.start()

    wait_rows(1, gwin)

    def adjoint_rows(low, high, rim):
        for g in range(WIDE // 16):
            span = slice(16 * g, 16 * g + 16)
            ks = [kb[8 - t, span, :] for t in range(9)]
            if rim:
                for b in range(3):
                    ks[6 + b] = jnp.where(top, kb[6 + b, span, :], ks[6 + b])

            def body(r):
                acc = cotan[r, span, :].astype(F32)
                for t in range(9):
                    acc = acc + ks[t] * gwin[t % 3, r + 2 * (t // 3), span, :]
                state_out[r, span, :] = (acc * mask[pl.ds(r, 1), :]).astype(BF)

            rows_loop(low, high, body, 2)

    adjoint_rows(0, ROWS // 2, False)
    for copy in lon_copies():
        copy.wait()
    total = part[lon_share(lon), :]
    for s in range(1, n_lon):
        total = total + lon_in[s]
    band[lon_share(lon), :] = total * scale

    def share_lon(s, source):
        piece = band.at[lon_share(source)]
        return rcopy(piece, piece, send_c.at[s], recv_c.at[s], lon=lon_peer(s))

    for s in range(1, n_lon):
        share_lon(s, lon).start()
    adjoint_rows(ROWS // 2, ROWS - 2, False)
    adjoint_rows(ROWS - 2, ROWS, True)
    for s in range(1, n_lon):
        share_lon(s, lon_peer(n_lon - s)).wait()
    whole[lat_share(lat), :] = band[...].astype(BF)

    def share_lat(s, source):
        piece = whole.at[lat_share(source)]
        return rcopy(piece, piece, send_d.at[s], recv_d.at[s], lat=lat_peer(s))

    for s in range(1, n_lat):
        share_lat(s, lat).start()
    for s in range(1, n_lat):
        share_lat(s, lat_peer(n_lat - s)).wait()
    final[...] = whole[...].astype(F32)

    def unpack(d, unused):
        start = pl.multiple_of(8 * d, 8)
        for which in range(2):
            for j in range(3):
                place = pl.ds(pl.multiple_of(8 * (57 * which + 3 * d + j), 8), 8)
                pad[which, pl.ds(start, 8), LANES * j : LANES * j + LANES] = final[place, :]
        return unused

    lax.fori_loop(0, 19, unpack, 0)
    for q in range(4):
        project_out[:, 75 * q : 75 * q + 75] = pad[0, :150, WIDE * q : WIDE * q + 75]
        expand_out[:, 75 * q : 75 * q + 75] = pad[1, :150, WIDE * q : WIDE * q + 75]
    bias_out[...] = pad[1, :, :LANES]
    kernel_out[...] = final[8 * TILES : 8 * (TILES + REST), :]


def on_device(
    ocean_state, land_mask, out_grad, swath_offset, swath_value,
    depth_kernel, expand_weight, expand_bias, project_weight,
):
    n_lon, n_lat = lax.axis_size("lon"), lax.axis_size("lat")
    channels = ocean_state.shape[0]
    units = expand_bias.shape[0]
    scale = 1.0 / math.sqrt(ROWS * n_lat * LANES * n_lon)
    extra = WIDE - channels

    def by_rows(x):
        return jnp.pad(jnp.transpose(x, (1, 0, 2)), ((0, 0), (0, extra), (0, 0)))


    def spread(w):
        w = w.reshape(units, 4, channels)
        return jnp.pad(w, ((0, UNITS - units), (0, 0), (0, extra)))

    high = lax.reduce_precision(expand_bias, 8, 7)
    middle = lax.reduce_precision(expand_bias - high, 8, 7)
    low = expand_bias - high - middle
    bias = jnp.stack([high, middle, low], axis=1).astype(BF)
    first = spread(expand_weight.T)
    bias = jnp.pad(bias[:, None, :], ((0, UNITS - units), (0, 3), (channels, extra - 3)))
    first = first + bias
    weights = jnp.stack([first, spread(project_weight)]).reshape(2, UNITS, 4 * WIDE)

    vmem = pl.BlockSpec(memory_space=pltpu.VMEM)
    block = (ROWS, WIDE, LANES)
    all_block = (4, SHARE, WIDE, LANES)
    all_rows = 8 * n_lat * n_lon
    dma = pltpu.SemaphoreType.DMA
    state, project, expand, bias_grad, kernel_grad = pl.pallas_call(
        functools.partial(step_kernel, scale, n_lon, n_lat),
        out_shape=[
            jax.ShapeDtypeStruct(block, BF),
            jax.ShapeDtypeStruct((units, 4 * channels), F32),
            jax.ShapeDtypeStruct((units, 4 * channels), F32),
            jax.ShapeDtypeStruct((152, LANES), F32),
            jax.ShapeDtypeStruct((WIDE, LANES), F32),
        ],
        in_specs=[vmem] * 7,
        out_specs=[vmem] * 5,
        scratch_shapes=[
            pltpu.VMEM((3, ROWS + 4, WIDE, LANES), F32),
            pltpu.VMEM((3, ROWS + 4, WIDE, LANES), F32),
            pltpu.VMEM((9, WIDE, LANES), F32),
            pltpu.VMEM((ROWS, LANES), F32),
            pltpu.VMEM((16, LANES), F32),
            pltpu.VMEM((ROWS, LANES), F32),
            pltpu.VMEM(block, BF),
            pltpu.VMEM(block, BF),
            pltpu.VMEM(all_block, BF),
            pltpu.VMEM(all_block, BF),
            pltpu.VMEM((4, 2, UNITS, 4 * WIDE), BF),
            pltpu.VMEM((2, WIDE, LANES), BF),
            pltpu.VMEM((2, 2, WIDE, LANES), BF),
            pltpu.VMEM((2, WIDE, LANES), F32),
            pltpu.VMEM((2, 2, 3, WIDE, LANES), BF),
            pltpu.VMEM((2, 2, 3, WIDE, LANES), BF),
            pltpu.VMEM((4 * UNITS, 3 * LANES), F32),
            pltpu.VMEM((4 * UNITS, 3 * LANES), F32),
            pltpu.VMEM(all_block, BF),
            pltpu.VMEM(block, BF),
            pltpu.VMEM((4, all_rows, LANES), F32),
            pltpu.VMEM((2, 8 * TILES, LANES), BF),
            pltpu.VMEM((2, 8 * TILES, LANES), BF),
            pltpu.VMEM((8 * TILES, LANES), BF),
            pltpu.VMEM((8 * TILES, LANES), BF),
            pltpu.VMEM((all_rows, LANES), BF),
            pltpu.VMEM((n_lat, 8 * n_lon, LANES), BF),
            pltpu.VMEM((8 * n_lon, LANES), F32),
            pltpu.VMEM((n_lon, 8, LANES), F32),
            pltpu.VMEM((8 * n_lon, LANES), F32),
            pltpu.VMEM((all_rows, LANES), BF),
            pltpu.VMEM((all_rows, LANES), F32),
            pltpu.VMEM((2, 152, 3 * LANES), F32),
        ]
        + [dma((2, 2))] * 4
        + [dma((3,))] * 2
        + [dma((4,))] * 2
        + [dma((4, 4))] * 4
        + [dma((2,))] * 2
        + [dma(())] * 2
        + [dma((n_lat,))] * 2
        + [dma((n_lon,))] * 4
        + [dma((n_lat,))] * 2,
        compiler_params=pltpu.CompilerParams(
            collective_id=0, has_side_effects=True, vmem_limit_bytes=56 * 2**20
        ),
    )(
        by_rows(ocean_state),
        by_rows(out_grad),
        land_mask,
        swath_offset.reshape(1, -1),
        swath_value.reshape(1, -1),
        depth_kernel,
        weights,
    )
    return (
        jnp.transpose(state[:, :channels], (1, 0, 2)),
        expand.T,
        project,
        bias_grad[:units, channels],
        kernel_grad[:channels, :9].T.reshape(3, 3, channels),
    )


def solution(mesh):
    return jax.shard_map(
        on_device,
        mesh=mesh,
        in_specs=(
            P("ch", "lat", "lon"),
            P("lat", "lon"),
            P("ch", "lat", "lon"),
            P("lat", "lon", None),
            P("lat", "lon", None),
            P(None, None, "ch"),
            P(None, "ch"),
            P("ch"),
            P("ch", None),
        ),
        out_specs=(
            P("ch", "lat", "lon"),
            P(None, "ch"),
            P("ch", None),
            P("ch"),
            P(None, None, "ch"),
        ),
        check_vma=False,
    )
```

```python
import functools
import math

import jax
import jax.numpy as jnp
from jax import lax
from jax.experimental import pallas as pl
from jax.experimental.pallas import tpu as pltpu
from jax.sharding import PartitionSpec as P

MESH = pl.DeviceIdType.MESH
ROWS = 32
WIDE = 80
LANES = 128
SHARE = 8
UNITS = 160
TILES = 114
REST = 10
BF = jnp.bfloat16
F32 = jnp.float32


def rcopy(src, dst, send, recv, **where):
    return pltpu.make_async_remote_copy(
        src, dst, send, recv, device_id=where, device_id_type=MESH
    )


def rows_loop(low, high, body, width=4):
    def several(n, unused):
        for t in range(width):
            body(low + n * width + t)
        return unused

    lax.fori_loop(0, (high - low) // width, several, 0)


def three_parts(x):
    high = x.astype(BF)
    left = x - high.astype(F32)
    middle = left.astype(BF)
    low = (left - middle.astype(F32)).astype(BF)
    return high, middle, low


def step_kernel(
    scale, n_lon, n_lat,
    state, grad, land, offset, value, taps, expand, project, bias,
    state_out, project_out, expand_out, bias_out, kernel_out,
    spread_out, weights, bias_row, turned, fwin, gwin, kb, mask, tap_rows, swath, cotan, conv, cot_all, conv_all, w_all,
    pack_out, pack_in, side, msg_out, msg_in,
    acc_p, acc_e, cg_out, cg_in, tiles, pair_out, pair_in, cross_out, cross_in,
    narrow, lat_in, part, lon_in, band, whole, final, pad,
    es, er, ms, mr, ws, wr, cs, cr, vs, vr, gs, gr, ps, pr, xs, xr,
    send_a, recv_a, send_b, recv_b, send_c, recv_c, send_d, recv_d,
):
    lon, lat, ch = lax.axis_index("lon"), lax.axis_index("lat"), lax.axis_index("ch")
    top = lat == n_lat - 1
    mate = ch + 1 - 2 * lax.rem(ch, 2)
    across = lax.rem(ch + 2, 4)
    mate_across = lax.rem(mate + 2, 4)
    far = lax.rem(lat + n_lat // 2, n_lat)
    lane = lax.broadcasted_iota(jnp.int32, (WIDE, LANES), 1)

    def lat_peer(step):
        return lax.rem(lat + step, n_lat)

    def lon_peer(step):
        return lax.rem(lon + step, n_lon)

    barrier = pltpu.get_barrier_semaphore()
    for step in range(1, n_lat):
        pl.semaphore_signal(barrier, inc=1, device_id={"lat": lat_peer(step)}, device_id_type=MESH)
    for step in range(1, n_lon):
        pl.semaphore_signal(barrier, inc=1, device_id={"lon": lon_peer(step)}, device_id_type=MESH)
    for step in range(1, 4):
        pl.semaphore_signal(
            barrier, inc=1, device_id={"ch": lax.rem(ch + step, 4)}, device_id_type=MESH
        )
    pl.semaphore_signal(
        barrier, inc=1, device_id={"ch": across, "lat": far}, device_id_type=MESH
    )

    def pack_edges(use, win):
        def body(r, acc):
            for t in range(4):
                row = 4 * r + t
                moved = pltpu.roll(win[1, 2 + row], lax.rem(4 * row + 2, LANES), 1)
                acc = jnp.where(lane // 4 == row, moved, acc)
            return acc

        pack_out[use] = lax.fori_loop(0, ROWS // 4, body, jnp.zeros((WIDE, LANES), F32)).astype(BF)

    def edge_copies(use):
        return [
            rcopy(pack_out.at[use], pack_in.at[use, 0], es.at[use, 0], er.at[use, 0], lon=lon_peer(1)),
            rcopy(pack_out.at[use], pack_in.at[use, 1], es.at[use, 1], er.at[use, 1], lon=lon_peer(n_lon - 1)),
        ]

    def send_edges(use):
        for copy in edge_copies(use):
            copy.start()

    def wait_edges(use):
        for copy in edge_copies(use):
            copy.wait()
        side[use] = jnp.where(
            lax.rem(lane, 4) < 2, pack_in[use, 0].astype(F32), pack_in[use, 1].astype(F32)
        )

    north_lat = jnp.minimum(lat + 1, n_lat - 1)
    north_lon = jnp.where(top, n_lon - 1 - lon, lon)
    north_slot = jnp.where(top, 1, 0)
    south_lat = jnp.maximum(lat - 1, 0)

    def north_copy(use):
        return rcopy(
            msg_out.at[use, 1], msg_in.at[use, north_slot], ms.at[use, 1], mr.at[use, north_slot],
            lat=north_lat, lon=north_lon,
        )

    def south_copy(use):
        return rcopy(
            msg_out.at[use, 0], msg_in.at[use, 1], ms.at[use, 0], mr.at[use, 1], lat=south_lat
        )

    def send_rows(use, win):
        edge = side[use]
        msg_out[use, 0, 0] = win[1, 2].astype(BF)
        msg_out[use, 0, 1] = win[1, 3].astype(BF)
        msg_out[use, 0, 2] = edge.astype(BF)

        @pl.when(lat > 0)
        def _():
            south_copy(use).start()

        @pl.when(jnp.logical_not(top))
        def _():
            msg_out[use, 1, 0] = win[1, ROWS].astype(BF)
            msg_out[use, 1, 1] = win[1, ROWS + 1].astype(BF)
            msg_out[use, 1, 2] = edge.astype(BF)

        @pl.when(top)
        def _():
            square = (LANES, LANES)
            turn = (
                lax.broadcasted_iota(jnp.int32, square, 0) + lax.broadcasted_iota(jnp.int32, square, 1)
                == LANES - 1
            ).astype(F32).astype(BF)
            for place, row in enumerate((win[1, ROWS + 1], win[1, ROWS], edge)):
                msg_out[use, 1, place] = jnp.dot(
                    row.astype(BF), turn, preferred_element_type=F32
                ).astype(BF)

        north_copy(use).start()

    def windows(win, p, quad, edge):
        x = win[1, p]
        win[0, p] = jnp.where(lane < 2, pltpu.roll(edge, lax.rem(LANES - 4 * quad, LANES), 1), pltpu.roll(x, 2, 1))
        win[2, p] = jnp.where(
            lane >= LANES - 2,
            pltpu.roll(edge, lax.rem(2 * LANES - 4 - 4 * quad, LANES), 1),
            pltpu.roll(x, LANES - 2, 1),
        )

    def inner_windows(use, win):
        edge = side[use]

        rows_loop(0, ROWS, lambda r: windows(win, r + 2, r, edge))

    def wait_rows(use, win):
        @pl.when(lat > 0)
        def _():
            south_copy(use).wait_send()
            rcopy(
                msg_out.at[use, 1], msg_in.at[use, 0], ms.at[use, 1], mr.at[use, 0], lat=south_lat
            ).wait_recv()

        @pl.when(lat == 0)
        def _():
            msg_in[use, 0] = jnp.zeros((3, WIDE, LANES), BF)

        north_copy(use).wait_send()
        rcopy(
            msg_out.at[use, 0], msg_in.at[use, 1], ms.at[use, 0], mr.at[use, 1],
            lat=north_lat, lon=north_lon,
        ).wait_recv()
        for slot, first, quad in ((0, 0, ROWS - 2), (1, ROWS + 2, 0)):
            edge = msg_in[use, slot, 2].astype(F32)
            for t in range(2):
                win[1, first + t] = msg_in[use, slot, t].astype(F32)
                windows(win, first + t, quad + t, edge)

    def scatter(q, src, dst, send, recv):
        @pl.when(ch != q)
        def _():
            rcopy(src, dst, send, recv, ch=jnp.int32(q)).start()

        @pl.when(ch == q)
        def _():
            dst[...] = src[...]

    def settle(q, src, dst, send, recv):
        @pl.when(ch != q)
        def _():
            rcopy(src, dst, send, recv, ch=jnp.int32(q)).wait()

    to_mate = rcopy(weights, w_all.at[ch], ws.at[0], wr.at[0], ch=mate)
    to_across = rcopy(weights, w_all.at[ch], ws.at[1], wr.at[1], ch=across, lat=far)
    passed = rcopy(w_all.at[across], w_all.at[across], ws.at[2], wr.at[2], ch=mate)
    mask[...] = land[...].astype(F32)
    pl.semaphore_wait(barrier, n_lat + n_lon + 2)

    def masked_rows(r):
        fwin[1, 2 + r] = state[r].astype(F32) * mask[pl.ds(r, 1), :]

    rows_loop(0, ROWS, masked_rows)
    pack_edges(0, fwin)
    send_edges(0)

    spot = offset[...]
    points = spot.shape[1]
    at_row = (
        lax.broadcasted_iota(jnp.int32, (ROWS, points), 0) == spot // LANES
    ).astype(F32).astype(BF)
    at_col = lax.broadcasted_iota(jnp.int32, (LANES, points), 0) == lax.rem(spot, LANES)
    spread = jnp.where(at_col, value[...], 0.0)
    total = jnp.zeros((ROWS, LANES), F32)
    for piece in three_parts(spread):
        total = total + lax.dot_general(
            at_row, piece, (((1,), (1,)), ((), ())), preferred_element_type=F32
        )
    swath[...] = total * jnp.where(ch == 0, 1.0, 0.0)

    first_channel = lax.broadcasted_iota(jnp.int32, (WIDE, LANES), 0) == 0

    def cotan_rows(r):
        row = grad[r].astype(F32)
        row = row + jnp.where(first_channel, swath[pl.ds(r, 1), :], 0.0)
        cotan[r] = (row * mask[pl.ds(r, 1), :]).astype(BF)

    rows_loop(0, ROWS, cotan_rows)
    for q in range(4):
        scatter(q, cotan.at[pl.ds(SHARE * q, SHARE)], cot_all.at[ch], cs.at[q], cr.at[ch])
    units, channels = project.shape[0], project.shape[1] // 4
    spread_out[...] = jnp.zeros_like(spread_out)
    bias_row[...] = jnp.zeros_like(bias_row)
    bias_row[0:1, :units] = bias[...]
    for which, ref in enumerate((expand, project)):
        full = ref[...].astype(F32)
        for q in range(4):
            spread_out[which, :units, WIDE * q : WIDE * q + channels] = full[:, channels * q : channels * q + channels]
    grid = (UNITS, 2 * LANES)
    same = lax.broadcasted_iota(jnp.int32, grid, 0) == lax.broadcasted_iota(jnp.int32, grid, 1)
    column = jnp.sum(jnp.where(same, bias_row[0:1, :], 0.0), axis=1, keepdims=True)
    for place, piece in enumerate(three_parts(column)):
        spread_out[0, :, channels + place : channels + place + 1] = piece.astype(F32)
    weights[...] = spread_out[:, :, : 4 * WIDE].astype(BF)
    to_across.start()
    to_mate.start()
    w_all[ch] = weights[...]
    tap_rows[...] = jnp.zeros_like(tap_rows)
    diagonal = lax.broadcasted_iota(jnp.int32, (WIDE, LANES), 0) == lane
    for t in range(9):
        tap_rows[t : t + 1, : taps.shape[2]] = taps[t // 3, t % 3 : t % 3 + 1, :]
    for t in range(9):
        column = jnp.where(diagonal, tap_rows[t : t + 1, :], 0.0)
        kb[t] = jnp.broadcast_to(jnp.sum(column, axis=1, keepdims=True), (WIDE, LANES))

    wait_edges(0)
    send_rows(0, fwin)
    inner_windows(0, fwin)
    to_across.wait()
    passed.start()

    def conv_piece(c):
        for g in range(WIDE // 16):
            span = slice(16 * g, 16 * g + 16)
            ks = [kb[t, span, :] for t in range(9)]
            for q in range(4):
                for r in (SHARE * q + 2 * c, SHARE * q + 2 * c + 1):
                    acc = ks[0] * fwin[0, r, span, :]
                    for t in range(1, 9):
                        acc = acc + ks[t] * fwin[t % 3, r + 2 * (t // 3), span, :]
                    if g == WIDE // 16 - 1:
                        unit = lax.broadcasted_iota(jnp.int32, (16, LANES), 0) + 16 * g
                        acc = jnp.where(unit >= 75, 1.0, acc)
                    conv[r, span, :] = acc.astype(BF)

    def conv_part(c, q):
        return conv.at[pl.ds(SHARE * q + 2 * c, 2)]

    def send_conv(c):
        for q in range(4):
            scatter(q, conv_part(c, q), conv_all.at[ch, pl.ds(2 * c, 2)], vs.at[c, q], vr.at[c, ch])

    for c in (1, 2):
        conv_piece(c)
        send_conv(c)
    wait_rows(0, fwin)
    for c in (3, 0):
        conv_piece(c)
        send_conv(c)

    to_mate.wait()
    acc_p[...] = jnp.zeros_like(acc_p)
    acc_e[...] = jnp.zeros_like(acc_e)
    rcopy(w_all.at[mate_across], w_all.at[mate_across], ws.at[2], wr.at[2], ch=mate).wait()
    for q in range(4):
        settle(q, cotan.at[pl.ds(SHARE * q, SHARE)], cot_all.at[q], cs.at[q], cr.at[q])

    c0 = math.sqrt(2.0 / math.pi)

    def back_part(c, q):
        return cg_out.at[q, pl.ds(2 * c, 2)]

    def cells(n, unused):
        c = lax.rem(n + 1, 4)
        for q in range(4):
            settle(q, conv_part(c, q), conv_all.at[q, pl.ds(2 * c, 2)], vs.at[c, q], vr.at[c, q])

        def both(ref):
            return jnp.concatenate(
                [
                    jnp.concatenate([ref[s, 2 * c + t] for s in range(4)], axis=0)
                    for t in range(2)
                ],
                axis=1,
            )

        x, y = both(conv_all), both(cot_all)
        w1 = w_all[:, 0].reshape(4 * UNITS, 4 * WIDE)
        w2 = w_all[:, 1].reshape(4 * UNITS, 4 * WIDE)
        h = jnp.dot(w1, x, preferred_element_type=F32)
        a = jnp.dot(w2, y, preferred_element_type=F32)
        square = h * h
        t = jnp.tanh(h * (c0 + (c0 * 0.044715) * square))
        half = 0.5 * t + 0.5
        activ = (h * half).astype(BF)
        slope = half + (0.5 * h) * (1.0 - t * t) * (c0 + (3.0 * c0 * 0.044715) * square)
        pre = (a * slope).astype(BF)
        acc_p[:, : 4 * WIDE] += lax.dot_general(activ, y, (((1,), (1,)), ((), ())), preferred_element_type=F32)
        acc_e[:, : 4 * WIDE] += lax.dot_general(pre, x, (((1,), (1,)), ((), ())), preferred_element_type=F32)
        back = lax.dot_general(w1, pre, (((0,), (0,)), ((), ())), preferred_element_type=F32).astype(BF)
        for q in range(4):
            for t in range(2):
                cg_out[q, 2 * c + t] = back[WIDE * q : WIDE * q + WIDE, LANES * t : LANES * t + LANES]
        for q in range(4):
            scatter(
                q, back_part(c, q), cg_in.at[pl.ds(SHARE * ch + 2 * c, 2)], gs.at[c, q], gr.at[c, ch]
            )
        return unused

    lax.fori_loop(0, SHARE // 2, cells, 0)

    for q in range(4):
        for which, ref in enumerate((acc_p, acc_e)):

            def body(d, unused):
                start = pl.multiple_of(UNITS * q + 8 * d, 8)
                for j in range(3):
                    place = pl.ds(pl.multiple_of(8 * (57 * which + 3 * d + j), 8), 8)
                    tiles[q, place, :] = ref[pl.ds(start, 8), LANES * j : LANES * j + LANES]
                return unused

            lax.fori_loop(0, 19, body, 0)

    used = pl.ds(0, 8 * TILES)
    pair_out[1] = tiles[mate_across, used, :].astype(BF)
    pair_out[0] = tiles[mate, used, :].astype(BF)
    pair = [
        rcopy(pair_out.at[1], pair_in.at[1], ps.at[1], pr.at[1], ch=mate),
        rcopy(pair_out.at[0], pair_in.at[0], ps.at[0], pr.at[0], ch=mate),
    ]
    for copy in pair:
        copy.start()

    for q in range(4):

        def body(c, unused):
            settle(q, back_part(c, q), cg_in.at[pl.ds(SHARE * q + 2 * c, 2)], gs.at[c, q], gr.at[c, q])
            return unused

        lax.fori_loop(0, SHARE // 2, body, 0)

    def grad_rows(r):
        gwin[1, 2 + r] = cg_in[r].astype(F32)

    rows_loop(0, ROWS, grad_rows)
    pack_edges(1, gwin)
    send_edges(1)

    def add_tiles(slot, ref, out=None):
        def body(d, unused):
            place = pl.ds(pl.multiple_of(48 * d, 16), 48)
            added = tiles[slot, place, :] + ref[place, :].astype(F32)
            if out is None:
                tiles[slot, place, :] = added
            else:
                out[place, :] = added.astype(BF)
            return unused

        lax.fori_loop(0, 8 * TILES // 48, body, 0)

    pair[0].wait()
    add_tiles(across, pair_in.at[1], cross_out)
    cross = rcopy(cross_out, cross_in, xs, xr, ch=across, lat=far)
    cross.start()
    pair[1].wait()
    add_tiles(ch, pair_in.at[0])

    for g in range(REST):
        span = slice(8 * g, 8 * g + 8)

        def body(n, sums):
            for u in range(4):
                r = 4 * n + u
                now = gwin[1, 2 + r, span, :]
                sums = tuple(
                    sums[t] + now * fwin[t % 3, r + 2 * (t // 3), span, :] for t in range(9)
                )
            return sums

        sums = lax.fori_loop(0, ROWS // 4, body, tuple(jnp.zeros((8, LANES), F32) for _ in range(9)))
        spots = lax.broadcasted_iota(jnp.int32, (8, LANES), 1)
        kept = jnp.zeros((8, LANES), F32)
        for t in range(9):
            kept = jnp.where(spots == t, jnp.sum(sums[t], axis=1, keepdims=True), kept)
        tiles[ch, 8 * (TILES + g) : 8 * (TILES + g) + 8, :] = kept
    spare = 8 * (n_lat * n_lon - TILES - REST)
    tiles[ch, 8 * (TILES + REST) :, :] = jnp.zeros((spare, LANES), F32)

    wait_edges(1)
    send_rows(1, gwin)
    cross.wait()
    add_tiles(ch, cross_in)
    share = 8 * n_lon

    def lat_share(place):
        return pl.ds(pl.multiple_of(share * place, 16), share)

    def lon_share(place):
        return pl.ds(pl.multiple_of(8 * place, 8), 8)

    narrow[...] = tiles[ch].astype(BF)

    def lat_copies():
        return [
            rcopy(narrow.at[lat_share(lat_peer(s))], lat_in.at[s], send_a.at[s], recv_a.at[s], lat=lat_peer(s))
            for s in range(1, n_lat)
        ]

    for copy in lat_copies():
        copy.start()

    inner_windows(1, gwin)
    for copy in lat_copies():
        copy.wait()
    total = tiles[ch, lat_share(lat), :]
    for s in range(1, n_lat):
        total = total + lat_in[s].astype(F32)
    part[...] = total

    def lon_copies():
        return [
            rcopy(part.at[lon_share(lon_peer(s))], lon_in.at[s], send_b.at[s], recv_b.at[s], lon=lon_peer(s))
            for s in range(1, n_lon)
        ]

    for copy in lon_copies():
        copy.start()

    wait_rows(1, gwin)

    def adjoint_rows(low, high, rim):
        for g in range(WIDE // 16):
            span = slice(16 * g, 16 * g + 16)
            ks = [kb[8 - t, span, :] for t in range(9)]
            if rim:
                for b in range(3):
                    ks[6 + b] = jnp.where(top, kb[6 + b, span, :], ks[6 + b])

            def body(r):
                acc = cotan[r, span, :].astype(F32)
                for t in range(9):
                    acc = acc + ks[t] * gwin[t % 3, r + 2 * (t // 3), span, :]
                state_out[r, span, :] = (acc * mask[pl.ds(r, 1), :]).astype(BF)

            rows_loop(low, high, body, 2)

    adjoint_rows(0, ROWS // 2, False)
    for copy in lon_copies():
        copy.wait()
    total = part[lon_share(lon), :]
    for s in range(1, n_lon):
        total = total + lon_in[s]
    band[lon_share(lon), :] = total * scale

    def share_lon(s, source):
        piece = band.at[lon_share(source)]
        return rcopy(piece, piece, send_c.at[s], recv_c.at[s], lon=lon_peer(s))

    for s in range(1, n_lon):
        share_lon(s, lon).start()
    adjoint_rows(ROWS // 2, ROWS - 2, False)
    adjoint_rows(ROWS - 2, ROWS, True)
    for s in range(1, n_lon):
        share_lon(s, lon_peer(n_lon - s)).wait()
    whole[lat_share(lat), :] = band[...].astype(BF)

    def share_lat(s, source):
        piece = whole.at[lat_share(source)]
        return rcopy(piece, piece, send_d.at[s], recv_d.at[s], lat=lat_peer(s))

    for s in range(1, n_lat):
        share_lat(s, lat).start()
    for s in range(1, n_lat):
        share_lat(s, lat_peer(n_lat - s)).wait()
    final[...] = whole[...].astype(F32)

    def unpack(d, unused):
        start = pl.multiple_of(8 * d, 8)
        for which in range(2):
            for j in range(3):
                place = pl.ds(pl.multiple_of(8 * (57 * which + 3 * d + j), 8), 8)
                pad[which, pl.ds(start, 8), LANES * j : LANES * j + LANES] = final[place, :]
        return unused

    lax.fori_loop(0, 19, unpack, 0)
    for q in range(4):
        project_out[:, 75 * q : 75 * q + 75] = pad[0, :150, WIDE * q : WIDE * q + 75]
        expand_out[:, 75 * q : 75 * q + 75] = pad[1, :150, WIDE * q : WIDE * q + 75]
    turned[...] = jnp.zeros_like(turned)
    turned[:152, :] = pad[1, :, :LANES]
    turned[2 * LANES : 2 * LANES + WIDE, :] = final[8 * TILES : 8 * (TILES + REST), :]
    flipped = jnp.transpose(turned[...])
    bias_out[...] = flipped[channels : channels + 1, :units]
    for t in range(9):
        kernel_out[t // 3, t % 3 : t % 3 + 1, :] = flipped[t : t + 1, 2 * LANES : 2 * LANES + channels]


def on_device(
    ocean_state, land_mask, out_grad, swath_offset, swath_value,
    depth_kernel, expand_weight, expand_bias, project_weight,
):
    n_lon, n_lat = lax.axis_size("lon"), lax.axis_size("lat")
    channels = ocean_state.shape[0]
    units = expand_bias.shape[0]
    scale = 1.0 / math.sqrt(ROWS * n_lat * LANES * n_lon)
    extra = WIDE - channels

    def by_rows(x):
        return jnp.pad(jnp.transpose(x, (1, 0, 2)), ((0, 0), (0, extra), (0, 0)))


    vmem = pl.BlockSpec(memory_space=pltpu.VMEM)
    block = (ROWS, WIDE, LANES)
    all_block = (4, SHARE, WIDE, LANES)
    all_rows = 8 * n_lat * n_lon
    dma = pltpu.SemaphoreType.DMA
    state, project, expand, bias_grad, kernel_grad = pl.pallas_call(
        functools.partial(step_kernel, scale, n_lon, n_lat),
        out_shape=[
            jax.ShapeDtypeStruct(block, BF),
            jax.ShapeDtypeStruct((units, 4 * channels), F32),
            jax.ShapeDtypeStruct((units, 4 * channels), F32),
            jax.ShapeDtypeStruct((1, units), F32),
            jax.ShapeDtypeStruct((3, 3, channels), F32),
        ],
        in_specs=[vmem] * 9,
        out_specs=[vmem] * 5,
        scratch_shapes=[
            pltpu.VMEM((2, UNITS, 3 * LANES), F32),
            pltpu.VMEM((2, UNITS, 4 * WIDE), BF),
            pltpu.VMEM((8, 2 * LANES), F32),
            pltpu.VMEM((3 * LANES, LANES), F32),
            pltpu.VMEM((3, ROWS + 4, WIDE, LANES), F32),
            pltpu.VMEM((3, ROWS + 4, WIDE, LANES), F32),
            pltpu.VMEM((9, WIDE, LANES), F32),
            pltpu.VMEM((ROWS, LANES), F32),
            pltpu.VMEM((16, LANES), F32),
            pltpu.VMEM((ROWS, LANES), F32),
            pltpu.VMEM(block, BF),
            pltpu.VMEM(block, BF),
            pltpu.VMEM(all_block, BF),
            pltpu.VMEM(all_block, BF),
            pltpu.VMEM((4, 2, UNITS, 4 * WIDE), BF),
            pltpu.VMEM((2, WIDE, LANES), BF),
            pltpu.VMEM((2, 2, WIDE, LANES), BF),
            pltpu.VMEM((2, WIDE, LANES), F32),
            pltpu.VMEM((2, 2, 3, WIDE, LANES), BF),
            pltpu.VMEM((2, 2, 3, WIDE, LANES), BF),
            pltpu.VMEM((4 * UNITS, 3 * LANES), F32),
            pltpu.VMEM((4 * UNITS, 3 * LANES), F32),
            pltpu.VMEM(all_block, BF),
            pltpu.VMEM(block, BF),
            pltpu.VMEM((4, all_rows, LANES), F32),
            pltpu.VMEM((2, 8 * TILES, LANES), BF),
            pltpu.VMEM((2, 8 * TILES, LANES), BF),
            pltpu.VMEM((8 * TILES, LANES), BF),
            pltpu.VMEM((8 * TILES, LANES), BF),
            pltpu.VMEM((all_rows, LANES), BF),
            pltpu.VMEM((n_lat, 8 * n_lon, LANES), BF),
            pltpu.VMEM((8 * n_lon, LANES), F32),
            pltpu.VMEM((n_lon, 8, LANES), F32),
            pltpu.VMEM((8 * n_lon, LANES), F32),
            pltpu.VMEM((all_rows, LANES), BF),
            pltpu.VMEM((all_rows, LANES), F32),
            pltpu.VMEM((2, 152, 3 * LANES), F32),
        ]
        + [dma((2, 2))] * 4
        + [dma((3,))] * 2
        + [dma((4,))] * 2
        + [dma((4, 4))] * 4
        + [dma((2,))] * 2
        + [dma(())] * 2
        + [dma((n_lat,))] * 2
        + [dma((n_lon,))] * 4
        + [dma((n_lat,))] * 2,
        compiler_params=pltpu.CompilerParams(
            collective_id=0, has_side_effects=True, vmem_limit_bytes=56 * 2**20
        ),
    )(
        by_rows(ocean_state),
        by_rows(out_grad),
        land_mask,
        swath_offset.reshape(1, -1),
        swath_value.reshape(1, -1),
        depth_kernel,
        expand_weight.T,
        project_weight,
        expand_bias.reshape(1, -1),
    )
    return (
        jnp.transpose(state[:, :channels], (1, 0, 2)),
        expand.T,
        project,
        bias_grad.reshape(-1),
        kernel_grad,
    )


def solution(mesh):
    return jax.shard_map(
        on_device,
        mesh=mesh,
        in_specs=(
            P("ch", "lat", "lon"),
            P("lat", "lon"),
            P("ch", "lat", "lon"),
            P("lat", "lon", None),
            P("lat", "lon", None),
            P(None, None, "ch"),
            P(None, "ch"),
            P("ch"),
            P("ch", None),
        ),
        out_specs=(
            P("ch", "lat", "lon"),
            P(None, "ch"),
            P("ch", None),
            P("ch"),
            P(None, None, "ch"),
        ),
        check_vma=False,
    )
```

```python
import functools
import math

import jax
import jax.numpy as jnp
from jax import lax
from jax.experimental import pallas as pl
from jax.experimental.pallas import tpu as pltpu
from jax.sharding import PartitionSpec as P

MESH = pl.DeviceIdType.MESH
ROWS = 32
WIDE = 80
LANES = 128
SHARE = 8
UNITS = 160
TILES = 114
REST = 10
BF = jnp.bfloat16
F32 = jnp.float32


def rcopy(src, dst, send, recv, **where):
    return pltpu.make_async_remote_copy(
        src, dst, send, recv, device_id=where, device_id_type=MESH
    )


def rows_loop(low, high, body, width=4):
    def several(n, unused):
        for t in range(width):
            body(low + n * width + t)
        return unused

    lax.fori_loop(0, (high - low) // width, several, 0)


def three_parts(x):
    high = x.astype(BF)
    left = x - high.astype(F32)
    middle = left.astype(BF)
    low = (left - middle.astype(F32)).astype(BF)
    return high, middle, low


def step_kernel(
    scale, n_lon, n_lat,
    state, grad, land, offset, value, taps, expand, project, bias,
    state_out, project_out, expand_out, bias_out, kernel_out,
    spread_out, weights, bias_row, turned, fwin, gwin, kb, mask, tap_rows, swath, cotan, conv, cot_all, conv_all, w_all,
    pack_out, pack_in, side, msg_out, msg_in,
    acc_p, acc_e, cg_out, cg_in, tiles, pair_out, pair_in, cross_out, cross_in,
    narrow, lat_in, part, lon_in, band, whole, final, pad,
    es, er, ms, mr, ws, wr, cs, cr, vs, vr, gs, gr, ps, pr, xs, xr,
    send_a, recv_a, send_b, recv_b, send_c, recv_c, send_d, recv_d,
):
    lon, lat, ch = lax.axis_index("lon"), lax.axis_index("lat"), lax.axis_index("ch")
    top = lat == n_lat - 1
    mate = ch + 1 - 2 * lax.rem(ch, 2)
    across = lax.rem(ch + 2, 4)
    mate_across = lax.rem(mate + 2, 4)
    far = lax.rem(lat + n_lat // 2, n_lat)
    lane = lax.broadcasted_iota(jnp.int32, (WIDE, LANES), 1)

    def lat_peer(step):
        return lax.rem(lat + step, n_lat)

    def lon_peer(step):
        return lax.rem(lon + step, n_lon)

    barrier = pltpu.get_barrier_semaphore()
    for step in range(1, n_lat):
        pl.semaphore_signal(barrier, inc=1, device_id={"lat": lat_peer(step)}, device_id_type=MESH)
    for step in range(1, n_lon):
        pl.semaphore_signal(barrier, inc=1, device_id={"lon": lon_peer(step)}, device_id_type=MESH)
    for step in range(1, 4):
        pl.semaphore_signal(
            barrier, inc=1, device_id={"ch": lax.rem(ch + step, 4)}, device_id_type=MESH
        )
    pl.semaphore_signal(
        barrier, inc=1, device_id={"ch": across, "lat": far}, device_id_type=MESH
    )

    def pack_edges(use, win):
        def body(r, acc):
            for t in range(4):
                row = 4 * r + t
                moved = pltpu.roll(win[1, 2 + row], lax.rem(4 * row + 2, LANES), 1)
                acc = jnp.where(lane // 4 == row, moved, acc)
            return acc

        pack_out[use] = lax.fori_loop(0, ROWS // 4, body, jnp.zeros((WIDE, LANES), F32)).astype(BF)

    def edge_copies(use):
        return [
            rcopy(pack_out.at[use], pack_in.at[use, 0], es.at[use, 0], er.at[use, 0], lon=lon_peer(1)),
            rcopy(pack_out.at[use], pack_in.at[use, 1], es.at[use, 1], er.at[use, 1], lon=lon_peer(n_lon - 1)),
        ]

    def send_edges(use):
        for copy in edge_copies(use):
            copy.start()

    def wait_edges(use):
        for copy in edge_copies(use):
            copy.wait()
        side[use] = jnp.where(
            lax.rem(lane, 4) < 2, pack_in[use, 0].astype(F32), pack_in[use, 1].astype(F32)
        )

    north_lat = jnp.minimum(lat + 1, n_lat - 1)
    north_lon = jnp.where(top, n_lon - 1 - lon, lon)
    north_slot = jnp.where(top, 1, 0)
    south_lat = jnp.maximum(lat - 1, 0)

    def north_copy(use):
        return rcopy(
            msg_out.at[use, 1], msg_in.at[use, north_slot], ms.at[use, 1], mr.at[use, north_slot],
            lat=north_lat, lon=north_lon,
        )

    def south_copy(use):
        return rcopy(
            msg_out.at[use, 0], msg_in.at[use, 1], ms.at[use, 0], mr.at[use, 1], lat=south_lat
        )

    def send_rows(use, win):
        edge = side[use]
        msg_out[use, 0, 0] = win[1, 2].astype(BF)
        msg_out[use, 0, 1] = win[1, 3].astype(BF)
        msg_out[use, 0, 2] = edge.astype(BF)

        @pl.when(lat > 0)
        def _():
            south_copy(use).start()

        @pl.when(jnp.logical_not(top))
        def _():
            msg_out[use, 1, 0] = win[1, ROWS].astype(BF)
            msg_out[use, 1, 1] = win[1, ROWS + 1].astype(BF)
            msg_out[use, 1, 2] = edge.astype(BF)

        @pl.when(top)
        def _():
            square = (LANES, LANES)
            turn = (
                lax.broadcasted_iota(jnp.int32, square, 0) + lax.broadcasted_iota(jnp.int32, square, 1)
                == LANES - 1
            ).astype(F32).astype(BF)
            for place, row in enumerate((win[1, ROWS + 1], win[1, ROWS], edge)):
                msg_out[use, 1, place] = jnp.dot(
                    row.astype(BF), turn, preferred_element_type=F32
                ).astype(BF)

        north_copy(use).start()

    def windows(win, p, quad, edge):
        x = win[1, p]
        win[0, p] = jnp.where(lane < 2, pltpu.roll(edge, lax.rem(LANES - 4 * quad, LANES), 1), pltpu.roll(x, 2, 1))
        win[2, p] = jnp.where(
            lane >= LANES - 2,
            pltpu.roll(edge, lax.rem(2 * LANES - 4 - 4 * quad, LANES), 1),
            pltpu.roll(x, LANES - 2, 1),
        )

    def inner_windows(use, win):
        edge = side[use]

        rows_loop(0, ROWS, lambda r: windows(win, r + 2, r, edge))

    def wait_rows(use, win):
        @pl.when(lat > 0)
        def _():
            south_copy(use).wait_send()
            rcopy(
                msg_out.at[use, 1], msg_in.at[use, 0], ms.at[use, 1], mr.at[use, 0], lat=south_lat
            ).wait_recv()

        @pl.when(lat == 0)
        def _():
            msg_in[use, 0] = jnp.zeros((3, WIDE, LANES), BF)

        north_copy(use).wait_send()
        rcopy(
            msg_out.at[use, 0], msg_in.at[use, 1], ms.at[use, 0], mr.at[use, 1],
            lat=north_lat, lon=north_lon,
        ).wait_recv()
        for slot, first, quad in ((0, 0, ROWS - 2), (1, ROWS + 2, 0)):
            edge = msg_in[use, slot, 2].astype(F32)
            for t in range(2):
                win[1, first + t] = msg_in[use, slot, t].astype(F32)
                windows(win, first + t, quad + t, edge)

    def scatter(q, src, dst, send, recv):
        @pl.when(ch != q)
        def _():
            rcopy(src, dst, send, recv, ch=jnp.int32(q)).start()

        @pl.when(ch == q)
        def _():
            dst[...] = src[...]

    def settle(q, src, dst, send, recv):
        @pl.when(ch != q)
        def _():
            rcopy(src, dst, send, recv, ch=jnp.int32(q)).wait()

    to_mate = rcopy(weights, w_all.at[ch], ws.at[0], wr.at[0], ch=mate)
    to_across = rcopy(weights, w_all.at[ch], ws.at[1], wr.at[1], ch=across, lat=far)
    passed = rcopy(w_all.at[across], w_all.at[across], ws.at[2], wr.at[2], ch=mate)
    mask[...] = land[...].astype(F32)
    pl.semaphore_wait(barrier, n_lat + n_lon + 2)

    def masked_rows(r):
        fwin[1, 2 + r] = state[r].astype(F32) * mask[pl.ds(r, 1), :]

    rows_loop(0, ROWS, masked_rows)
    pack_edges(0, fwin)
    send_edges(0)

    spot = offset[...]
    points = spot.shape[1]
    at_row = (
        lax.broadcasted_iota(jnp.int32, (ROWS, points), 0) == spot // LANES
    ).astype(F32).astype(BF)
    at_col = lax.broadcasted_iota(jnp.int32, (LANES, points), 0) == lax.rem(spot, LANES)
    spread = jnp.where(at_col, value[...], 0.0)
    total = jnp.zeros((ROWS, LANES), F32)
    for piece in three_parts(spread):
        total = total + lax.dot_general(
            at_row, piece, (((1,), (1,)), ((), ())), preferred_element_type=F32
        )
    swath[...] = total * jnp.where(ch == 0, 1.0, 0.0)

    first_channel = lax.broadcasted_iota(jnp.int32, (WIDE, LANES), 0) == 0

    def cotan_rows(r):
        row = grad[r].astype(F32)
        row = row + jnp.where(first_channel, swath[pl.ds(r, 1), :], 0.0)
        cotan[r] = (row * mask[pl.ds(r, 1), :]).astype(BF)

    rows_loop(0, ROWS, cotan_rows)
    for q in range(4):
        scatter(q, cotan.at[pl.ds(SHARE * q, SHARE)], cot_all.at[ch], cs.at[q], cr.at[ch])
    wait_edges(0)
    send_rows(0, fwin)
    units, channels = project.shape[0], project.shape[1] // 4
    spread_out[...] = jnp.zeros_like(spread_out)
    bias_row[...] = jnp.zeros_like(bias_row)
    bias_row[0:1, :units] = bias[...]
    for which, ref in enumerate((expand, project)):
        full = ref[...].astype(F32)
        for q in range(4):
            spread_out[which, :units, WIDE * q : WIDE * q + channels] = full[:, channels * q : channels * q + channels]
    grid = (UNITS, 2 * LANES)
    same = lax.broadcasted_iota(jnp.int32, grid, 0) == lax.broadcasted_iota(jnp.int32, grid, 1)
    column = jnp.sum(jnp.where(same, bias_row[0:1, :], 0.0), axis=1, keepdims=True)
    for place, piece in enumerate(three_parts(column)):
        spread_out[0, :, channels + place : channels + place + 1] = piece.astype(F32)
    weights[...] = spread_out[:, :, : 4 * WIDE].astype(BF)
    to_across.start()
    to_mate.start()
    w_all[ch] = weights[...]
    tap_rows[...] = jnp.zeros_like(tap_rows)
    diagonal = lax.broadcasted_iota(jnp.int32, (WIDE, LANES), 0) == lane
    for t in range(9):
        tap_rows[t : t + 1, : taps.shape[2]] = taps[t // 3, t % 3 : t % 3 + 1, :]
    for t in range(9):
        column = jnp.where(diagonal, tap_rows[t : t + 1, :], 0.0)
        kb[t] = jnp.broadcast_to(jnp.sum(column, axis=1, keepdims=True), (WIDE, LANES))

    inner_windows(0, fwin)

    def conv_piece(c):
        for g in range(WIDE // 16):
            span = slice(16 * g, 16 * g + 16)
            ks = [kb[t, span, :] for t in range(9)]
            for q in range(4):
                for r in (SHARE * q + 2 * c, SHARE * q + 2 * c + 1):
                    acc = ks[0] * fwin[0, r, span, :]
                    for t in range(1, 9):
                        acc = acc + ks[t] * fwin[t % 3, r + 2 * (t // 3), span, :]
                    if g == WIDE // 16 - 1:
                        unit = lax.broadcasted_iota(jnp.int32, (16, LANES), 0) + 16 * g
                        acc = jnp.where(unit >= 75, 1.0, acc)
                    conv[r, span, :] = acc.astype(BF)

    def conv_part(c, q):
        return conv.at[pl.ds(SHARE * q + 2 * c, 2)]

    def send_conv(c):
        for q in range(4):
            scatter(q, conv_part(c, q), conv_all.at[ch, pl.ds(2 * c, 2)], vs.at[c, q], vr.at[c, ch])

    for c in (1, 2):
        conv_piece(c)
        send_conv(c)
    wait_rows(0, fwin)
    for c in (3, 0):
        conv_piece(c)
        send_conv(c)
    to_across.wait()
    passed.start()

    to_mate.wait()
    acc_p[...] = jnp.zeros_like(acc_p)
    acc_e[...] = jnp.zeros_like(acc_e)
    rcopy(w_all.at[mate_across], w_all.at[mate_across], ws.at[2], wr.at[2], ch=mate).wait()
    for q in range(4):
        settle(q, cotan.at[pl.ds(SHARE * q, SHARE)], cot_all.at[q], cs.at[q], cr.at[q])

    c0 = math.sqrt(2.0 / math.pi)

    def back_part(c, q):
        return cg_out.at[q, pl.ds(2 * c, 2)]

    def cells(n, unused):
        c = lax.rem(n + 1, 4)
        for q in range(4):
            settle(q, conv_part(c, q), conv_all.at[q, pl.ds(2 * c, 2)], vs.at[c, q], vr.at[c, q])

        def both(ref):
            return jnp.concatenate(
                [
                    jnp.concatenate([ref[s, 2 * c + t] for s in range(4)], axis=0)
                    for t in range(2)
                ],
                axis=1,
            )

        x, y = both(conv_all), both(cot_all)
        w1 = w_all[:, 0].reshape(4 * UNITS, 4 * WIDE)
        w2 = w_all[:, 1].reshape(4 * UNITS, 4 * WIDE)
        h = jnp.dot(w1, x, preferred_element_type=F32)
        a = jnp.dot(w2, y, preferred_element_type=F32)
        square = h * h
        t = jnp.tanh(h * (c0 + (c0 * 0.044715) * square))
        half = 0.5 * t + 0.5
        activ = (h * half).astype(BF)
        slope = half + (0.5 * h) * (1.0 - t * t) * (c0 + (3.0 * c0 * 0.044715) * square)
        pre = (a * slope).astype(BF)
        acc_p[:, : 4 * WIDE] += lax.dot_general(activ, y, (((1,), (1,)), ((), ())), preferred_element_type=F32)
        acc_e[:, : 4 * WIDE] += lax.dot_general(pre, x, (((1,), (1,)), ((), ())), preferred_element_type=F32)
        back = lax.dot_general(w1, pre, (((0,), (0,)), ((), ())), preferred_element_type=F32).astype(BF)
        for q in range(4):
            for t in range(2):
                cg_out[q, 2 * c + t] = back[WIDE * q : WIDE * q + WIDE, LANES * t : LANES * t + LANES]
        for q in range(4):
            scatter(
                q, back_part(c, q), cg_in.at[pl.ds(SHARE * ch + 2 * c, 2)], gs.at[c, q], gr.at[c, ch]
            )
        return unused

    lax.fori_loop(0, SHARE // 2, cells, 0)

    for q in range(4):
        for which, ref in enumerate((acc_p, acc_e)):

            def body(d, unused):
                start = pl.multiple_of(UNITS * q + 8 * d, 8)
                for j in range(3):
                    place = pl.ds(pl.multiple_of(8 * (57 * which + 3 * d + j), 8), 8)
                    tiles[q, place, :] = ref[pl.ds(start, 8), LANES * j : LANES * j + LANES]
                return unused

            lax.fori_loop(0, 19, body, 0)

    used = pl.ds(0, 8 * TILES)
    pair_out[1] = tiles[mate_across, used, :].astype(BF)
    pair_out[0] = tiles[mate, used, :].astype(BF)
    pair = [
        rcopy(pair_out.at[1], pair_in.at[1], ps.at[1], pr.at[1], ch=mate),
        rcopy(pair_out.at[0], pair_in.at[0], ps.at[0], pr.at[0], ch=mate),
    ]
    for copy in pair:
        copy.start()

    for q in range(4):

        def body(c, unused):
            settle(q, back_part(c, q), cg_in.at[pl.ds(SHARE * q + 2 * c, 2)], gs.at[c, q], gr.at[c, q])
            return unused

        lax.fori_loop(0, SHARE // 2, body, 0)

    def grad_rows(r):
        gwin[1, 2 + r] = cg_in[r].astype(F32)

    rows_loop(0, ROWS, grad_rows)
    pack_edges(1, gwin)
    send_edges(1)

    def add_tiles(slot, ref, out=None):
        def body(d, unused):
            place = pl.ds(pl.multiple_of(48 * d, 16), 48)
            added = tiles[slot, place, :] + ref[place, :].astype(F32)
            if out is None:
                tiles[slot, place, :] = added
            else:
                out[place, :] = added.astype(BF)
            return unused

        lax.fori_loop(0, 8 * TILES // 48, body, 0)

    pair[0].wait()
    add_tiles(across, pair_in.at[1], cross_out)
    cross = rcopy(cross_out, cross_in, xs, xr, ch=across, lat=far)
    cross.start()
    pair[1].wait()
    add_tiles(ch, pair_in.at[0])

    for g in range(REST):
        span = slice(8 * g, 8 * g + 8)

        def body(n, sums):
            for u in range(4):
                r = 4 * n + u
                now = gwin[1, 2 + r, span, :]
                sums = tuple(
                    sums[t] + now * fwin[t % 3, r + 2 * (t // 3), span, :] for t in range(9)
                )
            return sums

        sums = lax.fori_loop(0, ROWS // 4, body, tuple(jnp.zeros((8, LANES), F32) for _ in range(9)))
        spots = lax.broadcasted_iota(jnp.int32, (8, LANES), 1)
        kept = jnp.zeros((8, LANES), F32)
        for t in range(9):
            kept = jnp.where(spots == t, jnp.sum(sums[t], axis=1, keepdims=True), kept)
        tiles[ch, 8 * (TILES + g) : 8 * (TILES + g) + 8, :] = kept
    spare = 8 * (n_lat * n_lon - TILES - REST)
    tiles[ch, 8 * (TILES + REST) :, :] = jnp.zeros((spare, LANES), F32)

    wait_edges(1)
    send_rows(1, gwin)
    cross.wait()
    add_tiles(ch, cross_in)
    share = 8 * n_lon

    def lat_share(place):
        return pl.ds(pl.multiple_of(share * place, 16), share)

    def lon_share(place):
        return pl.ds(pl.multiple_of(8 * place, 8), 8)

    narrow[...] = tiles[ch].astype(BF)

    def lat_copies():
        return [
            rcopy(narrow.at[lat_share(lat_peer(s))], lat_in.at[s], send_a.at[s], recv_a.at[s], lat=lat_peer(s))
            for s in range(1, n_lat)
        ]

    for copy in lat_copies():
        copy.start()

    inner_windows(1, gwin)
    for copy in lat_copies():
        copy.wait()
    total = tiles[ch, lat_share(lat), :]
    for s in range(1, n_lat):
        total = total + lat_in[s].astype(F32)
    part[...] = total

    def lon_copies():
        return [
            rcopy(part.at[lon_share(lon_peer(s))], lon_in.at[s], send_b.at[s], recv_b.at[s], lon=lon_peer(s))
            for s in range(1, n_lon)
        ]

    for copy in lon_copies():
        copy.start()

    wait_rows(1, gwin)

    def adjoint_rows(low, high, rim):
        for g in range(WIDE // 16):
            span = slice(16 * g, 16 * g + 16)
            ks = [kb[8 - t, span, :] for t in range(9)]
            if rim:
                for b in range(3):
                    ks[6 + b] = jnp.where(top, kb[6 + b, span, :], ks[6 + b])

            def body(r):
                acc = cotan[r, span, :].astype(F32)
                for t in range(9):
                    acc = acc + ks[t] * gwin[t % 3, r + 2 * (t // 3), span, :]
                state_out[r, span, :] = (acc * mask[pl.ds(r, 1), :]).astype(BF)

            rows_loop(low, high, body, 2)

    adjoint_rows(0, ROWS // 2, False)
    for copy in lon_copies():
        copy.wait()
    total = part[lon_share(lon), :]
    for s in range(1, n_lon):
        total = total + lon_in[s]
    band[lon_share(lon), :] = total * scale

    def share_lon(s, source):
        piece = band.at[lon_share(source)]
        return rcopy(piece, piece, send_c.at[s], recv_c.at[s], lon=lon_peer(s))

    for s in range(1, n_lon):
        share_lon(s, lon).start()
    adjoint_rows(ROWS // 2, ROWS - 2, False)
    adjoint_rows(ROWS - 2, ROWS, True)
    for s in range(1, n_lon):
        share_lon(s, lon_peer(n_lon - s)).wait()
    whole[lat_share(lat), :] = band[...].astype(BF)

    def share_lat(s, source):
        piece = whole.at[lat_share(source)]
        return rcopy(piece, piece, send_d.at[s], recv_d.at[s], lat=lat_peer(s))

    for s in range(1, n_lat):
        share_lat(s, lat).start()
    for s in range(1, n_lat):
        share_lat(s, lat_peer(n_lat - s)).wait()
    final[...] = whole[...].astype(F32)

    def unpack(d, unused):
        start = pl.multiple_of(8 * d, 8)
        for which in range(2):
            for j in range(3):
                place = pl.ds(pl.multiple_of(8 * (57 * which + 3 * d + j), 8), 8)
                pad[which, pl.ds(start, 8), LANES * j : LANES * j + LANES] = final[place, :]
        return unused

    lax.fori_loop(0, 19, unpack, 0)
    for q in range(4):
        project_out[:, 75 * q : 75 * q + 75] = pad[0, :150, WIDE * q : WIDE * q + 75]
        expand_out[:, 75 * q : 75 * q + 75] = pad[1, :150, WIDE * q : WIDE * q + 75]
    turned[...] = jnp.zeros_like(turned)
    turned[:152, :] = pad[1, :, :LANES]
    turned[2 * LANES : 2 * LANES + WIDE, :] = final[8 * TILES : 8 * (TILES + REST), :]
    flipped = jnp.transpose(turned[...])
    bias_out[...] = flipped[channels : channels + 1, :units]
    for t in range(9):
        kernel_out[t // 3, t % 3 : t % 3 + 1, :] = flipped[t : t + 1, 2 * LANES : 2 * LANES + channels]


def on_device(
    ocean_state, land_mask, out_grad, swath_offset, swath_value,
    depth_kernel, expand_weight, expand_bias, project_weight,
):
    n_lon, n_lat = lax.axis_size("lon"), lax.axis_size("lat")
    channels = ocean_state.shape[0]
    units = expand_bias.shape[0]
    scale = 1.0 / math.sqrt(ROWS * n_lat * LANES * n_lon)
    extra = WIDE - channels

    def by_rows(x):
        return jnp.pad(jnp.transpose(x, (1, 0, 2)), ((0, 0), (0, extra), (0, 0)))


    vmem = pl.BlockSpec(memory_space=pltpu.VMEM)
    block = (ROWS, WIDE, LANES)
    all_block = (4, SHARE, WIDE, LANES)
    all_rows = 8 * n_lat * n_lon
    dma = pltpu.SemaphoreType.DMA
    state, project, expand, bias_grad, kernel_grad = pl.pallas_call(
        functools.partial(step_kernel, scale, n_lon, n_lat),
        out_shape=[
            jax.ShapeDtypeStruct(block, BF),
            jax.ShapeDtypeStruct((units, 4 * channels), F32),
            jax.ShapeDtypeStruct((units, 4 * channels), F32),
            jax.ShapeDtypeStruct((1, units), F32),
            jax.ShapeDtypeStruct((3, 3, channels), F32),
        ],
        in_specs=[vmem] * 9,
        out_specs=[vmem] * 5,
        scratch_shapes=[
            pltpu.VMEM((2, UNITS, 3 * LANES), F32),
            pltpu.VMEM((2, UNITS, 4 * WIDE), BF),
            pltpu.VMEM((8, 2 * LANES), F32),
            pltpu.VMEM((3 * LANES, LANES), F32),
            pltpu.VMEM((3, ROWS + 4, WIDE, LANES), F32),
            pltpu.VMEM((3, ROWS + 4, WIDE, LANES), F32),
            pltpu.VMEM((9, WIDE, LANES), F32),
            pltpu.VMEM((ROWS, LANES), F32),
            pltpu.VMEM((16, LANES), F32),
            pltpu.VMEM((ROWS, LANES), F32),
            pltpu.VMEM(block, BF),
            pltpu.VMEM(block, BF),
            pltpu.VMEM(all_block, BF),
            pltpu.VMEM(all_block, BF),
            pltpu.VMEM((4, 2, UNITS, 4 * WIDE), BF),
            pltpu.VMEM((2, WIDE, LANES), BF),
            pltpu.VMEM((2, 2, WIDE, LANES), BF),
            pltpu.VMEM((2, WIDE, LANES), F32),
            pltpu.VMEM((2, 2, 3, WIDE, LANES), BF),
            pltpu.VMEM((2, 2, 3, WIDE, LANES), BF),
            pltpu.VMEM((4 * UNITS, 3 * LANES), F32),
            pltpu.VMEM((4 * UNITS, 3 * LANES), F32),
            pltpu.VMEM(all_block, BF),
            pltpu.VMEM(block, BF),
            pltpu.VMEM((4, all_rows, LANES), F32),
            pltpu.VMEM((2, 8 * TILES, LANES), BF),
            pltpu.VMEM((2, 8 * TILES, LANES), BF),
            pltpu.VMEM((8 * TILES, LANES), BF),
            pltpu.VMEM((8 * TILES, LANES), BF),
            pltpu.VMEM((all_rows, LANES), BF),
            pltpu.VMEM((n_lat, 8 * n_lon, LANES), BF),
            pltpu.VMEM((8 * n_lon, LANES), F32),
            pltpu.VMEM((n_lon, 8, LANES), F32),
            pltpu.VMEM((8 * n_lon, LANES), F32),
            pltpu.VMEM((all_rows, LANES), BF),
            pltpu.VMEM((all_rows, LANES), F32),
            pltpu.VMEM((2, 152, 3 * LANES), F32),
        ]
        + [dma((2, 2))] * 4
        + [dma((3,))] * 2
        + [dma((4,))] * 2
        + [dma((4, 4))] * 4
        + [dma((2,))] * 2
        + [dma(())] * 2
        + [dma((n_lat,))] * 2
        + [dma((n_lon,))] * 4
        + [dma((n_lat,))] * 2,
        compiler_params=pltpu.CompilerParams(
            collective_id=0, has_side_effects=True, vmem_limit_bytes=56 * 2**20
        ),
    )(
        by_rows(ocean_state),
        by_rows(out_grad),
        land_mask,
        swath_offset.reshape(1, -1),
        swath_value.reshape(1, -1),
        depth_kernel,
        expand_weight.T,
        project_weight,
        expand_bias.reshape(1, -1),
    )
    return (
        jnp.transpose(state[:, :channels], (1, 0, 2)),
        expand.T,
        project,
        bias_grad.reshape(-1),
        kernel_grad,
    )


def solution(mesh):
    return jax.shard_map(
        on_device,
        mesh=mesh,
        in_specs=(
            P("ch", "lat", "lon"),
            P("lat", "lon"),
            P("ch", "lat", "lon"),
            P("lat", "lon", None),
            P("lat", "lon", None),
            P(None, None, "ch"),
            P(None, "ch"),
            P("ch"),
            P("ch", None),
        ),
        out_specs=(
            P("ch", "lat", "lon"),
            P(None, "ch"),
            P("ch", None),
            P("ch"),
            P(None, None, "ch"),
        ),
        check_vma=False,
    )
```
